32 devices in a mesh: seq: 16 (over z, y, x), head: 2 (over core).
Axes of the slice: x: 2, y: 2, z: 4, core: 2. Of those that a mesh axis runs over, the one named last changes fastest.
Arguments:
- queries: bfloat16 [2048, 16, 128], P('seq', 'head'), may hold values from -6 to 6
- key_vectors: bfloat16 [2048, 16, 128], P('seq', 'head'), may hold values from -16 to 16
- values: bfloat16 [2048, 16, 128], P('seq', 'head'), may hold values from -6 to 6
- out_gate: bfloat16 [2048, 16, 128], P('seq', 'head'), may hold values from -6 to 6
- inputs: bfloat16 [2048, 2048], P('seq', 'head'), may hold values from -6 to 6
- beta_weight: bfloat16 [16, 2048], P(None, 'head'), may hold values from -0.1875 to 0.1875
- log_decay: float32 [16, 2048], P('head', 'seq'), may hold values from -1 to 0
- initial_state: float32 [16, 128, 128], P('head'), may hold values from -6 to 6
Outputs:
- gated_out: bfloat16 [2048, 16, 128], P('seq', 'head')
- block_states: float32 [32, 16, 128, 128], P('seq', 'head')
The draws below stay inside these ranges and needn't reach their ends.
All inputs are finite; a program needn't handle non-finite values.
Results may differ from the reference program's by a relative error of at most 0.0012.
Values sent between devices are 32-bit elements; how exact they have to be, the bound alone decides.
No kernel may reach another device: no remote copies, remote signals or barrier semaphores. Data moves between devices by JAX's collectives and lax.ppermute only.
A program may use at most 64 MiB of HBM per device.

```python
import math
import jax
import jax.numpy as jnp
from jax import lax

D = 2048
HEADS = 16
HEAD_DIM = 128
BLOCK = 64
TOK_DEV = 128
SEQUENCE_TOKENS = 2048


def gradual_heads(key, slow_count):
    ranking = jax.random.permutation(jax.random.fold_in(key, 41), HEADS)
    return ranking < slow_count


def draw_key_vectors(key, part):
    rough_key = jax.random.fold_in(jax.random.fold_in(key, 17), 0)
    entry_key = jax.random.fold_in(jax.random.fold_in(key, 17), 1)
    basis_key = jax.random.fold_in(jax.random.fold_in(key, 17), 3)
    position = jnp.arange(SEQUENCE_TOKENS, dtype=jnp.float32)
    rising = jnp.sqrt(1.0 + 2.0 * position / SEQUENCE_TOKENS)[:, None, None]
    roughness = jnp.exp(jax.random.uniform(rough_key, (SEQUENCE_TOKENS, HEADS, 1), minval=-1.2, maxval=1.2))
    slow_count = HEADS // 2
    entries = jax.random.normal(entry_key, (SEQUENCE_TOKENS, HEADS, HEAD_DIM), dtype=jnp.float32)
    gradual = gradual_heads(key, slow_count)
    orders = jax.vmap(lambda head_key: jax.random.permutation(head_key, HEAD_DIM))(jax.random.split(basis_key, HEADS))
    inside = orders < HEAD_DIM // 4
    leakage = math.sqrt(HEAD_DIM / (4.0 * SEQUENCE_TOKENS))
    column_scale = jnp.where(jnp.logical_or(inside, jnp.logical_not(gradual[:, None])), 1.0, leakage)
    return jnp.clip(entries * column_scale[None] * roughness * rising, -16.0, 16.0).astype(jnp.bfloat16)


def draw_log_decay(key, part):
    slow_key = jax.random.fold_in(jax.random.fold_in(key, 29), 1)
    fast_key = jax.random.fold_in(jax.random.fold_in(key, 29), 2)
    token_key = jax.random.fold_in(jax.random.fold_in(key, 29), 3)
    block_key = jax.random.fold_in(jax.random.fold_in(key, 29), 4)
    place_key = jax.random.fold_in(jax.random.fold_in(key, 29), 5)
    depth_key = jax.random.fold_in(jax.random.fold_in(key, 29), 6)
    slow_count = HEADS // 2
    gradual = gradual_heads(key, slow_count)[:, None]
    slow_rate = jnp.exp(jax.random.uniform(slow_key, (HEADS, 1), minval=math.log(0.05 / SEQUENCE_TOKENS), maxval=math.log(0.5 / SEQUENCE_TOKENS)))
    fast_rate = jnp.exp(jax.random.uniform(fast_key, (HEADS, 1), minval=math.log(1.0 / 50.0), maxval=math.log(1.0 / 30.0)))
    baseline_decay_rate = jnp.where(gradual, slow_rate, fast_rate)
    token_scale_factor = jnp.exp(jax.random.uniform(token_key, (HEADS, SEQUENCE_TOKENS), minval=-0.7, maxval=0.7))
    block_scale_factor = jnp.repeat(jnp.exp(jax.random.uniform(block_key, (HEADS, SEQUENCE_TOKENS // TOK_DEV), minval=-0.7, maxval=0.7)), TOK_DEV, axis=1)
    spike_positions = jax.random.randint(place_key, (3,), 0, SEQUENCE_TOKENS)
    decay_depths = jax.random.uniform(depth_key, (3, HEADS), minval=0.2, maxval=0.5)
    spike_region_mask = (jnp.arange(SEQUENCE_TOKENS)[None, :] == spike_positions[:, None]).astype(jnp.float32)
    spike_regions = jnp.einsum('gn,gs->ns', jnp.log(1.0 - decay_depths), spike_region_mask)
    return -baseline_decay_rate * token_scale_factor * block_scale_factor + jnp.where(gradual, spike_regions, 0.0)


def spiked(values, own_key, source, target, blocks, factor):
    def block_of(axis_at):
        return (jnp.arange(values.shape[axis_at]) // (values.shape[axis_at] // blocks)).reshape((-1,) + (1,) * (values.ndim - 1 - axis_at))

    one_side = jax.random.permutation(own_key, blocks)[block_of(target)]
    second = (block_of(target) + blocks // 2) % blocks
    return jnp.where((block_of(source) == one_side) | (block_of(source) == second), factor * values, values)


def steps_of(own_key, extent, cuts, low, largest):
    level = 1.0
    for axis_at, blocks in cuts:
        heights = jax.random.uniform(jax.random.fold_in(jax.random.fold_in(own_key, 6), axis_at), (blocks,), jnp.float32, low / len(cuts), largest / len(cuts))
        level = level * jnp.repeat(jnp.exp(heights), extent[axis_at] // blocks).reshape((-1,) + (1,) * (len(extent) - 1 - axis_at))
    return level


def bell_draw(key, dims, width, most, pieces=(), kind=jnp.bfloat16):
    drawn = width * jax.random.normal(key, dims, jnp.float32)
    if pieces:
        drawn = drawn * steps_of(key, dims, pieces, -0.22, 0.18)
    return jnp.clip(drawn, -most, most).astype(kind)


def gaussian_with(key, dims, scale, limit, cuts, heavy, held_as=jnp.bfloat16):
    array = scale * jax.random.normal(key, dims, jnp.float32)
    if cuts:
        array = array * steps_of(key, dims, cuts, -0.22, 0.18)
    return jnp.clip(spiked(array, jax.random.fold_in(key, 3), *heavy), -limit, limit).astype(held_as)


def setup_inputs(seed: int = 0) -> dict:
    key_list = jax.random.split(jax.random.key(seed), 9)
    return {
        "queries": bell_draw(key_list[0], (SEQUENCE_TOKENS, HEADS, HEAD_DIM), 1.0, 6.0, ((0, 16), (1, 2))),
        "key_vectors": draw_key_vectors(jax.random.fold_in(key_list[8], 71), 0),
        "values": bell_draw(key_list[2], (SEQUENCE_TOKENS, HEADS, HEAD_DIM), 1.0, 6.0, ((0, 16), (1, 2))),
        "out_gate": bell_draw(key_list[3], (SEQUENCE_TOKENS, HEADS, HEAD_DIM), 1.0, 6.0, ((0, 16), (1, 2))),
        "inputs": bell_draw(key_list[4], (SEQUENCE_TOKENS, D), 1.0, 6.0, ((0, 16), (1, 2))),
        "beta_weight": gaussian_with(key_list[5], (HEADS, D), D ** -0.5, 0.1875, ((1, 2),), (1, 0, 2, 2.0)),
        "log_decay": draw_log_decay(jax.random.fold_in(key_list[8], 71), 0),
        "initial_state": bell_draw(key_list[7], (HEADS, HEAD_DIM, HEAD_DIM), 1.0, 6.0, ((0, 2),), jnp.float32),
    }


EPSILON = 1e-06

def matmul(matrix, operand):
    return jnp.einsum('...ij,...jk->...ik', matrix, operand, precision=lax.Precision.HIGHEST)

def normalize(query_block, key_block, key_limit):
    query_float = query_block.astype(jnp.float32)
    key_float = key_block.astype(jnp.float32)
    queries_unit = query_float / jnp.sqrt(lax.optimization_barrier(jnp.sum(query_float * query_float, -1, keepdims=True)) + EPSILON) * query_float.shape[-1] ** (-0.5)
    keys_unit = key_float / jnp.maximum(jnp.sqrt(lax.optimization_barrier(jnp.sum(key_float * key_float, -1, keepdims=True))), key_limit)
    return (queries_unit, keys_unit)

def block_parts(queries_unit, keys_unit, value_rows, beta_gate, decay_rows):
    length = decay_rows.shape[-1]
    feature = keys_unit.shape[-1]
    cumulative = jnp.cumsum(decay_rows, axis=-1)
    inside = jnp.tril(jnp.ones((length, length), jnp.float32))
    strict = jnp.tril(jnp.ones((length, length), jnp.float32), -1)
    spread = jnp.where(inside > 0, cumulative[..., :, None] - cumulative[..., None, :], 0.0)
    damping = jnp.exp(spread) * inside
    intersections = jnp.einsum('...id,...jd->...ij', keys_unit, keys_unit, precision=lax.Precision.HIGHEST)
    system = jnp.eye(length, dtype=jnp.float32) + beta_gate[..., :, None] * intersections * damping * strict
    right_side = jnp.concatenate([(beta_gate * jnp.exp(cumulative))[..., None] * keys_unit, beta_gate[..., None] * value_rows], axis=-1)
    solved = lax.linalg.triangular_solve(system, right_side, left_side=True, lower=True, unit_diagonal=True)
    write_keys = solved[..., :feature]
    write_values = solved[..., feature:]
    final_sum = cumulative[..., -1:]
    carried = keys_unit * jnp.exp(final_sum - cumulative)[..., None]
    transition = jnp.exp(final_sum)[..., None] * jnp.eye(feature, dtype=jnp.float32) - jnp.einsum('...ld,...le->...de', carried, write_keys, precision=lax.Precision.HIGHEST)
    offset = jnp.einsum('...ld,...le->...de', carried, write_values, precision=lax.Precision.HIGHEST)
    reached = queries_unit * jnp.exp(cumulative)[..., None]
    scores = jnp.einsum('...id,...jd->...ij', queries_unit, keys_unit, precision=lax.Precision.HIGHEST) * damping
    return (write_keys, write_values, transition, offset, reached, scores)

def block_out(block_info, state_now):
    write_keys, write_values, transition, offset, reached, scores = block_info
    corrected = write_values - matmul(write_keys, state_now)
    return matmul(reached, state_now) + matmul(scores, corrected)

def gate_norm(raw_out, gate_rows):
    inverse_rms = 1.0 / jnp.sqrt(lax.optimization_barrier(jnp.mean(raw_out * raw_out, -1, keepdims=True)) + EPSILON)
    return (raw_out * inverse_rms * jax.nn.silu(gate_rows.astype(jnp.float32))).astype(jnp.bfloat16)

def reference(queries, key_vectors, values, out_gate, inputs, beta_weight, log_decay, initial_state):
    token_count = queries.shape[0]
    head_count = queries.shape[1]
    logits = lax.dot_general(beta_weight.astype(jnp.float32), inputs.astype(jnp.float32), (((1,), (1,)), ((), ())), preferred_element_type=jnp.float32)
    beta_gate = jax.nn.sigmoid(logits)
    key_float = key_vectors.astype(jnp.float32)
    key_total = lax.optimization_barrier(jnp.sum(key_float * key_float, axis=(0, 2)))
    key_limit = jnp.sqrt(key_total / token_count + EPSILON)
    blocks = token_count // BLOCK

    def arrange(tensor):
        return tensor.reshape(blocks, BLOCK, head_count, -1).transpose(0, 2, 1, 3)

    def arrange_rows(tensor):
        return tensor.reshape(head_count, blocks, BLOCK).transpose(1, 0, 2)
    sources = (arrange(queries), arrange(key_vectors), arrange(values), arrange(out_gate), arrange_rows(beta_gate), arrange_rows(log_decay))

    def step(state_now, source):
        query_block, key_block, value_block, gate_block, beta_block, decay_block = source
        queries_unit, keys_unit = normalize(query_block, key_block, key_limit[:, None, None])
        block_info = block_parts(queries_unit, keys_unit, value_block.astype(jnp.float32), beta_block, decay_block)
        raw_out = block_out(block_info, state_now)
        following = matmul(block_info[2], state_now) + block_info[3]
        return (following, (gate_norm(raw_out, gate_block), state_now))
    _, (outputs, states) = lax.scan(step, initial_state.astype(jnp.float32), sources)
    gated_out = outputs.transpose(0, 2, 1, 3).reshape(token_count, head_count, -1)
    return (gated_out, states)
```

```python
import functools
import math

import jax
import jax.numpy as jnp
from jax import lax
from jax.experimental import pallas as pl
from jax.experimental.pallas import tpu as pltpu
from jax.sharding import PartitionSpec as P

BLOCK = 64
EPSILON = 1e-06
F32 = jnp.float32
BF16 = jnp.bfloat16
VMEM_LIMIT = 56 * 1024 * 1024


def split(x):
    high = x.astype(BF16)
    return high, (x - high.astype(F32)).astype(BF16)


def mm(a, b):
    return jnp.dot(a, b, preferred_element_type=F32)


def dot_split(left, right):
    (lh, ll), (rh, rl) = left, right
    return mm(jnp.concatenate([lh, ll], 1), jnp.concatenate([rh, rh], 0)) + mm(lh, rl)


def dot_square(left, right):
    (lh, ll), (rh, rl) = left, right
    n = rh.shape[1]
    wide = mm(
        jnp.concatenate([lh, ll], 1),
        jnp.concatenate(
            [jnp.concatenate([rh, rl], 1), jnp.concatenate([rh, jnp.zeros_like(rl)], 1)], 0
        ),
    )
    return wide[:, :n] + wide[:, n:]


def iotas(n, m):
    return (
        lax.broadcasted_iota(jnp.int32, (n, m), 0),
        lax.broadcasted_iota(jnp.int32, (n, m), 1),
    )


def vmem(count):
    return [pl.BlockSpec(memory_space=pltpu.VMEM)] * count


def smem():
    return pl.BlockSpec(memory_space=pltpu.SMEM)


def call(kernel, out_shape, scratch=(), scalars=0, operands=0, flops=0, name=None):
    single = not isinstance(out_shape, (list, tuple))
    return pl.pallas_call(
        kernel,
        out_shape=out_shape,
        in_specs=[smem()] * scalars + vmem(operands),
        out_specs=vmem(1)[0] if single else vmem(len(out_shape)),
        scratch_shapes=list(scratch),
        compiler_params=pltpu.CompilerParams(vmem_limit_bytes=VMEM_LIMIT),
        cost_estimate=pl.CostEstimate(flops=flops, bytes_accessed=1 << 20, transcendentals=0),
        name=name,
    )


def shape(*dims, dtype=F32):
    return jax.ShapeDtypeStruct(dims, dtype)


def stats_kernel(heads, key_ref, weight_ref, inputs_ref, total_ref, logits_ref):
    keys = key_ref[...].astype(F32)
    squares = keys * keys
    rows = squares.shape[0]
    total = squares.reshape(rows // heads, heads, squares.shape[1]).sum(0)
    total_ref[...] = total
    logits_ref[...] = lax.dot_general(
        weight_ref[...], inputs_ref[...], (((1,), (1,)), ((), ())), preferred_element_type=F32
    )


def gather_rows(source_ref, rows_ref, order, at):
    for item, head in enumerate(order):
        rows_ref[at + item : at + item + 1, :] = source_ref[pl.ds(head, 1), :]


def item_heads(rank_ref, groups, per):
    return [(slot ^ rank_ref[0]) * per + i for slot in range(groups) for i in range(per)]


def solve_kernel(
    groups,
    per,
    tokens_all,
    rank_ref,
    key_ref,
    value_ref,
    logit_ref,
    total_ref,
    decay_ref,
    maps_ref,
    wu_ref,
    cum_ref,
    flat_ref,
    rows_ref,
):
    heads = groups * per
    n = decay_ref.shape[1]
    d = key_ref.shape[1]
    order = item_heads(rank_ref, groups, per)
    row, col = iotas(n, n)
    lane = lax.broadcasted_iota(jnp.int32, (heads, n), 1)

    cum = decay_ref[...]
    step = 1
    while step < n:
        cum = cum + jnp.where(lane >= step, pltpu.roll(cum, step, 1), 0.0)
        step *= 2
    cum_ref[...] = cum
    limit = jnp.sqrt(jnp.sum(total_ref[...], 1, keepdims=True) / tokens_all + EPSILON)

    flat_ref[...] = key_ref[...].astype(F32)
    keys, keys_t, grams = [], [], []
    for item, head in enumerate(order):
        key = flat_ref[pl.ds(head, n, stride=heads), :].astype(BF16)
        keys.append(key)
        keys_t.append(key.T)
    for item in range(heads):
        gram = mm(keys[item], keys_t[item])
        grams.append(gram)
        rows_ref[item : item + 1, :] = jnp.sum(jnp.where(row == col, gram, 0.0), 0, keepdims=True)
    gather_rows(cum_ref, rows_ref, order, heads)
    rows_ref[2 * heads : 3 * heads, :] = 1.0 / (1.0 + jnp.exp(-logit_ref[...]))
    rows_ref[3 * heads : 4 * heads, :] = jnp.broadcast_to(limit, (heads, n))
    gather_rows(rows_ref, rows_ref, [2 * heads + h for h in order], 4 * heads)
    gather_rows(rows_ref, rows_ref, [3 * heads + h for h in order], 5 * heads)
    norm = rows_ref[0:heads, :]
    cum = rows_ref[heads : 2 * heads, :]
    beta = rows_ref[4 * heads : 5 * heads, :]
    inverse = 1.0 / jnp.maximum(jnp.sqrt(norm), rows_ref[5 * heads : 6 * heads, :])
    last = cum[:, n - 1 : n]
    carry = inverse * jnp.exp(last - cum)
    lift = jnp.exp(last)
    rows_ref[6 * heads : 7 * heads, :] = beta * inverse
    rows_ref[7 * heads : 8 * heads, :] = carry
    columns = rows_ref[...].T

    def column(kind, item):
        at = kind * heads + item
        return columns[:, at : at + 1]

    systems, inverses = [], []
    for item in range(heads):
        spread = column(1, item) - cum[item : item + 1, :]
        damping = jnp.exp(jnp.where(row > col, spread, 0.0))
        system = jnp.where(
            row > col,
            grams[item] * damping * column(6, item) * inverse[item : item + 1, :],
            0.0,
        )
        systems.append(split(system))
        inverses.append(
            jnp.where(row == col, 1.0, jnp.where((row ^ col) == 1, -system, 0.0))
        )
    size = 2
    while size < n:
        joins = ((row ^ col) & ~(2 * size - 1)) == 0
        joins = joins & ((row & size) != 0) & ((col & size) == 0)
        parts = [split(x) for x in inverses]
        mids = [split(dot_square(a, x)) for a, x in zip(systems, parts)]
        ends = [dot_square(x, t) for x, t in zip(parts, mids)]
        inverses = [x - jnp.where(joins, e, 0.0) for x, e in zip(inverses, ends)]
        size *= 2

    flat_ref[...] = value_ref[...].astype(F32)
    write_scale = beta * jnp.exp(cum) * inverse
    for item, head in enumerate(order):
        x = inverses[item]
        value = flat_ref[pl.ds(head, n, stride=heads), :].astype(BF16)
        key = keys[item]
        w = mm(
            jnp.concatenate(split(x * write_scale[item : item + 1, :]), 1),
            jnp.concatenate([key, key], 0),
        )
        u = mm(
            jnp.concatenate(split(x * beta[item : item + 1, :]), 1),
            jnp.concatenate([value, value], 0),
        )
        wu = jnp.concatenate([w, u], 1)
        wu_ref[item] = wu
        scaled = split(wu * column(7, item))
        both = mm(
            jnp.concatenate([keys_t[item], keys_t[item]], 1), jnp.concatenate(scaled, 0)
        )
        ends = jnp.where(row == col, lift[item : item + 1, :], 0.0)
        maps_ref[item // per, item % per] = jnp.concatenate([ends - both[:, :d], both[:, d:]], 1)


def output_kernel(
    groups,
    per,
    tokens_all,
    rank_ref,
    query_ref,
    key_ref,
    total_ref,
    cum_ref,
    wu_ref,
    left_ref,
    right_ref,
    flat_ref,
    rows_ref,
):
    heads = groups * per
    n = cum_ref.shape[1]
    d = key_ref.shape[1]
    blocks = n // BLOCK
    order = item_heads(rank_ref, groups, per)
    row, col = iotas(n, n)
    limit = jnp.sqrt(jnp.sum(total_ref[...], 1, keepdims=True) / tokens_all + EPSILON)
    rows_ref[0:heads, :] = jnp.broadcast_to(limit, (heads, n))
    gather_rows(rows_ref, rows_ref, order, heads)
    gather_rows(cum_ref, rows_ref, order, 2 * heads)
    limit = rows_ref[heads : 2 * heads, :]
    cum = rows_ref[2 * heads : 3 * heads, :]
    flat_ref[...] = key_ref[...].astype(F32)
    keys = [flat_ref[pl.ds(head, n, stride=heads), :] for head in order]
    flat_ref[...] = query_ref[...].astype(F32)
    queries = [flat_ref[pl.ds(head, n, stride=heads), :] for head in order]
    norms = []
    for item in range(heads):
        norms.append(jnp.sum(keys[item] * keys[item], 1, keepdims=True))
    position = lax.broadcasted_iota(jnp.int32, (heads, n), 1)
    kinds = [cum]
    for b in range(1, blocks):
        end = b * BLOCK
        kinds.append(
            jnp.where(position < end, jnp.exp(jnp.minimum(cum[:, end - 1 : end] - cum, 0.0)), 0.0)
        )
    kinds.append(limit)
    for at, kind in enumerate(kinds):
        rows_ref[at * heads : (at + 1) * heads, :] = kind
    columns = rows_ref[...].T
    spare = len(kinds) * heads
    inverse_columns = [
        1.0
        / jnp.maximum(
            jnp.sqrt(norms[item]),
            columns[:, (len(kinds) - 1) * heads + item : (len(kinds) - 1) * heads + item + 1],
        )
        for item in range(heads)
    ]
    for item in range(heads):
        wu = wu_ref[item]
        key = keys[item].astype(BF16)
        key_t = key.T
        query = queries[item]
        cum_column = columns[:, item : item + 1]
        inverse = inverse_columns[item]
        reach = (
            1.0
            / jnp.sqrt(jnp.sum(query * query, 1, keepdims=True) + EPSILON)
            * (d**-0.5)
        )
        scores = mm(query.astype(BF16), key_t)
        spread = jnp.where(row >= col, cum_column - cum[item : item + 1, :], 0.0)
        scores = jnp.where(row >= col, scores * jnp.exp(spread), 0.0) * reach
        scaled = split(wu * inverse)
        both = dot_split(split(scores), scaled)
        rest = [query * (reach * jnp.exp(cum_column)) - both[:, :d]]
        outs = [both[:, d:]]
        for b in range(1, blocks):
            carry = columns[:, b * heads + item : b * heads + item + 1]
            part = split(wu * (inverse * carry))
            inner = mm(jnp.concatenate([key_t, key_t], 1), jnp.concatenate(part, 0))
            at = b * BLOCK - 1
            ends = jnp.where(row == col, jnp.exp(cum[item : item + 1, at : at + 1]), 0.0)
            rest.append(ends - inner[:, :d])
            outs.append(inner[:, d:])
        left_ref[item] = jnp.concatenate(split(jnp.concatenate(rest, 0)), 1)
        right_ref[item] = jnp.concatenate(outs, 0)


def join(latter, earlier):
    d = latter.shape[0]
    both = dot_split(split(latter[:, :d]), split(earlier))
    return jnp.concatenate([both[:, :d], both[:, d:] + latter[:, d:]], 1)


def apply(step, state):
    d = state.shape[0]
    return dot_split(split(step[:, :d]), split(state)) + step[:, d:]


def compose_kernel(groups, per, rank_ref, *refs):
    parts, (prefix_ref, total_ref, held_ref) = refs[:groups], refs[groups:]
    for slot in range(groups):
        held_ref[slot ^ rank_ref[0]] = parts[slot][...]
    so_far = [held_ref[0, i] for i in range(per)]
    for place in range(1, groups):
        for i in range(per):
            prefix_ref[place - 1, i] = so_far[i]
        so_far = [join(held_ref[place, i], so_far[i]) for i in range(per)]
    for i in range(per):
        total_ref[i] = so_far[i]


def middle_kernel(per, upper_ref, mine_ref, other_ref, start_ref, state_ref):
    for i in range(per):
        mine, other = mine_ref[i], other_ref[i]
        upper = upper_ref[0] != 0
        earlier = jnp.where(upper, other, mine)
        latter = jnp.where(upper, mine, other)
        state_ref[i] = apply(latter, apply(earlier, start_ref[i]))


def enter_kernel(
    groups, per, rank_ref, upper_ref, later_ref, prefix_ref, before_ref, start_ref, came_ref, out_ref
):
    for i in range(per):
        state = jnp.where(later_ref[0] != 0, came_ref[i], start_ref[i])
        moved = apply(before_ref[i], state)
        state = jnp.where(upper_ref[0] != 0, moved, state)
        out_ref[rank_ref[0], i] = state
        for place in range(1, groups):
            out_ref[place ^ rank_ref[0], i] = apply(prefix_ref[place - 1, i], state)


def finish_kernel(groups, per, rank_ref, *refs):
    states = refs[:groups]
    left_ref, right_ref, gate_ref, out_ref, block_ref, flat_ref, gates_ref = refs[groups:]
    heads = groups * per
    order = item_heads(rank_ref, groups, per)
    d = gate_ref.shape[1]
    n = gate_ref.shape[0] // heads
    blocks = block_ref.shape[0]
    gates_ref[...] = gate_ref[...].astype(F32)
    for item, head in enumerate(order):
        state = states[item // per][item % per]
        high, low = split(state)
        left = left_ref[item]
        both = mm(left, jnp.concatenate([high, high], 0)) + mm(left[:, :d], low) + right_ref[item]
        raw = both[:n]
        block_ref[0, head] = state
        for b in range(1, blocks):
            block_ref[b, head] = both[n + (b - 1) * d : n + b * d]
        gate = gates_ref[pl.ds(head, n, stride=heads), :]
        scale = 1.0 / jnp.sqrt(jnp.mean(raw * raw, 1, keepdims=True) + EPSILON)
        flat_ref[pl.ds(head, n, stride=heads), :] = raw * scale * (gate / (1.0 + jnp.exp(-gate)))
    out_ref[...] = flat_ref[...].astype(BF16)


def exact(matrix, operand):
    return jnp.einsum("...ij,...jk->...ik", matrix, operand, precision=lax.Precision.HIGHEST)


def chain(latter, earlier):
    d = latter.shape[-2]
    both = exact(latter[..., :d], earlier)
    return jnp.concatenate([both[..., :d], both[..., d:] + latter[..., d:]], -1)


def flag(value):
    return jnp.reshape(value, (1,)).astype(jnp.int32)


def on_device(
    queries, key_vectors, values, out_gate, inputs, beta_weight, log_decay, initial_state
):
    n, heads, d = queries.shape
    blocks = n // BLOCK
    count, place = lax.axis_size("seq"), lax.axis_index("seq")
    groups = math.gcd(math.gcd(4, heads), count)
    per = heads // groups
    runs = count // groups
    rounds = runs.bit_length() - 1
    assert runs == 1 << rounds
    rank = flag(place % groups)
    run = place // groups

    def flipped(mask):
        return [(i, i ^ mask) for i in range(count)]

    def flat(tensor):
        return tensor.reshape(n * heads, d)

    total, logits = call(
        functools.partial(stats_kernel, heads),
        (shape(heads, d), shape(beta_weight.shape[0], n)),
        operands=3,
        name="stats",
    )(flat(key_vectors), beta_weight, inputs)
    if lax.axis_size("head") == 2:
        side = lax.axis_index("head")
        halves = logits.reshape(2, heads, n)
        own = lax.dynamic_index_in_dim(halves, side, 0, keepdims=False)
        theirs = lax.dynamic_index_in_dim(halves, 1 - side, 0, keepdims=False)
        logits = own + lax.ppermute(theirs, "head", [(0, 1), (1, 0)])
    else:
        logits = lax.psum_scatter(logits, "head", scatter_dimension=0, tiled=True)
    mask = 1
    while mask < count:
        total = total + lax.ppermute(total, "seq", flipped(mask))
        mask *= 2

    tokens_all = n * count
    maps, wu, cum = call(
        functools.partial(solve_kernel, groups, per, tokens_all),
        (shape(groups, per, d, 2 * d), shape(heads, n, 2 * d), shape(heads, n)),
        scratch=(pltpu.VMEM((n * heads, d), F32), pltpu.VMEM((128, n), F32)),
        scalars=1,
        operands=5,
        flops=1 << 30,
        name="solve",
    )(rank, flat(key_vectors), flat(values), logits, total, log_decay)

    parts = [maps[0]] + [
        lax.ppermute(maps[slot], "seq", flipped(slot)) for slot in range(1, groups)
    ]
    left, right = call(
        functools.partial(output_kernel, groups, per, tokens_all),
        (shape(heads, n + (blocks - 1) * d, 2 * d, dtype=BF16), shape(heads, n + (blocks - 1) * d, d)),
        scratch=(pltpu.VMEM((n * heads, d), F32), pltpu.VMEM((128, n), F32)),
        scalars=1,
        operands=5,
        flops=1 << 30,
        name="outputs",
    )(rank, flat(queries), flat(key_vectors), total, cum, wu)

    prefix, run_map = call(
        functools.partial(compose_kernel, groups, per),
        (shape(max(groups - 1, 1), per, d, 2 * d), shape(per, d, 2 * d)),
        scratch=(pltpu.VMEM((groups, per, d, 2 * d), F32),),
        scalars=1,
        operands=groups,
        flops=1 << 27,
        name="compose",
    )(rank, *parts)
    start = lax.dynamic_slice_in_dim(initial_state, (place % groups) * per, per, 0)

    before, upper, came, later = run_map, flag(0), start, flag(0)
    if rounds == 2:
        other = lax.ppermute(run_map, "seq", flipped(groups))
        upper = flag(run & 1)
        before = other
        middle = call(
            functools.partial(middle_kernel, per),
            shape(per, d, d),
            scalars=1,
            operands=3,
            name="middle",
        )(upper, run_map, other, start)
    elif rounds:
        eye = jnp.broadcast_to(jnp.eye(d, 2 * d, dtype=F32), run_map.shape)
        before, upper, window = eye, flag(1), run_map
        for r in range(rounds - 1):
            other = lax.ppermute(window, "seq", flipped(groups << r))
            high = (run >> r) & 1 == 1
            before = jnp.where(high, chain(before, other), before)
            window = chain(jnp.where(high, window, other), jnp.where(high, other, window))
        middle = exact(window[..., :d], start) + window[..., d:]
    if rounds:
        half = count // 2
        came = lax.ppermute(middle, "seq", [(i, i + half) for i in range(half)])
        later = flag(run >= runs // 2)
    entries = call(
        functools.partial(enter_kernel, groups, per),
        shape(groups, per, d, d),
        scalars=3,
        operands=4,
        flops=1 << 27,
        name="enter",
    )(rank, upper, later, prefix, before, start, came)

    states = [entries[0]] + [
        lax.ppermute(entries[slot], "seq", flipped(slot)) for slot in range(1, groups)
    ]
    gated, block_states = call(
        functools.partial(finish_kernel, groups, per),
        (shape(n * heads, d, dtype=BF16), shape(blocks, heads, d, d)),
        scratch=(pltpu.VMEM((n * heads, d), F32), pltpu.VMEM((n * heads, d), F32)),
        scalars=1,
        operands=groups + 3,
        flops=1 << 28,
        name="finish",
    )(rank, *states, left, right, flat(out_gate))
    return (gated.reshape(n, heads, d), block_states)


def solution(mesh):
    return jax.shard_map(
        on_device,
        mesh=mesh,
        in_specs=(
            P("seq", "head", None),
            P("seq", "head", None),
            P("seq", "head", None),
            P("seq", "head", None),
            P("seq", "head"),
            P(None, "head"),
            P("head", "seq"),
            P("head", None, None),
        ),
        out_specs=(P("seq", "head", None), P("seq", "head", None, None)),
        check_vma=False,
    )
```

```python
import functools
import math

import jax
import jax.numpy as jnp
from jax import lax
from jax.experimental import pallas as pl
from jax.experimental.pallas import tpu as pltpu
from jax.sharding import PartitionSpec as P

BLOCK = 64
EPSILON = 1e-06
F32 = jnp.float32
BF16 = jnp.bfloat16
VMEM_LIMIT = 20 * 1024 * 1024


def split(x):
    high = x.astype(BF16)
    return high, (x - high.astype(F32)).astype(BF16)


def mm(a, b):
    return jnp.dot(a, b, preferred_element_type=F32)


def dot_split(left, right):
    (lh, ll), (rh, rl) = left, right
    return mm(jnp.concatenate([lh, ll], 1), jnp.concatenate([rh, rh], 0)) + mm(lh, rl)


def dot_square(left, right):
    (lh, ll), (rh, rl) = left, right
    n = rh.shape[1]
    wide = mm(
        jnp.concatenate([lh, ll], 1),
        jnp.concatenate(
            [jnp.concatenate([rh, rl], 1), jnp.concatenate([rh, jnp.zeros_like(rl)], 1)], 0
        ),
    )
    return wide[:, :n] + wide[:, n:]


def iotas(n, m):
    return (
        lax.broadcasted_iota(jnp.int32, (n, m), 0),
        lax.broadcasted_iota(jnp.int32, (n, m), 1),
    )


def vmem(count):
    return [pl.BlockSpec(memory_space=pltpu.VMEM)] * count


def smem():
    return pl.BlockSpec(memory_space=pltpu.SMEM)


def call(kernel, out_shape, scratch=(), scalars=0, operands=0, flops=0, name=None):
    single = not isinstance(out_shape, (list, tuple))
    return pl.pallas_call(
        kernel,
        out_shape=out_shape,
        in_specs=[smem()] * scalars + vmem(operands),
        out_specs=vmem(1)[0] if single else vmem(len(out_shape)),
        scratch_shapes=list(scratch),
        compiler_params=pltpu.CompilerParams(vmem_limit_bytes=VMEM_LIMIT),
        cost_estimate=pl.CostEstimate(flops=flops, bytes_accessed=1 << 20, transcendentals=0),
        name=name,
    )


def shape(*dims, dtype=F32):
    return jax.ShapeDtypeStruct(dims, dtype)


def stats_kernel(heads, key_ref, weight_ref, inputs_ref, total_ref, logits_ref):
    keys = key_ref[...].astype(F32)
    squares = keys * keys
    rows = squares.shape[0]
    total = squares.reshape(rows // heads, heads, squares.shape[1]).sum(0)
    total_ref[...] = total
    logits_ref[...] = lax.dot_general(
        weight_ref[...], inputs_ref[...], (((1,), (1,)), ((), ())), preferred_element_type=F32
    )


def gather_rows(source_ref, rows_ref, order, at):
    for item, head in enumerate(order):
        rows_ref[at + item : at + item + 1, :] = source_ref[pl.ds(head, 1), :]


def item_heads(rank_ref, groups, per):
    return [(slot ^ rank_ref[0]) * per + i for slot in range(groups) for i in range(per)]


def solve_kernel(
    groups,
    per,
    tokens_all,
    rank_ref,
    key_ref,
    value_ref,
    logit_ref,
    total_ref,
    decay_ref,
    *refs,
):
    maps_refs, (wu_ref, cum_ref, flat_ref, rows_ref) = refs[:groups], refs[groups:]
    heads = groups * per
    n = decay_ref.shape[1]
    d = key_ref.shape[1]
    order = item_heads(rank_ref, groups, per)
    row, col = iotas(n, n)
    lane = lax.broadcasted_iota(jnp.int32, (heads, n), 1)

    cum = decay_ref[...]
    step = 1
    while step < n:
        cum = cum + jnp.where(lane >= step, pltpu.roll(cum, step, 1), 0.0)
        step *= 2
    cum_ref[...] = cum
    limit = jnp.sqrt(jnp.sum(total_ref[...], 1, keepdims=True) / tokens_all + EPSILON)

    flat_ref[...] = key_ref[...].astype(F32)
    keys, keys_t, grams = [], [], []
    for item, head in enumerate(order):
        key = flat_ref[pl.ds(head, n, stride=heads), :].astype(BF16)
        keys.append(key)
        keys_t.append(key.T)
    for item in range(heads):
        gram = mm(keys[item], keys_t[item])
        grams.append(gram)
        rows_ref[item : item + 1, :] = jnp.sum(jnp.where(row == col, gram, 0.0), 0, keepdims=True)
    gather_rows(cum_ref, rows_ref, order, heads)
    rows_ref[2 * heads : 3 * heads, :] = 1.0 / (1.0 + jnp.exp(-logit_ref[...]))
    rows_ref[3 * heads : 4 * heads, :] = jnp.broadcast_to(limit, (heads, n))
    gather_rows(rows_ref, rows_ref, [2 * heads + h for h in order], 4 * heads)
    gather_rows(rows_ref, rows_ref, [3 * heads + h for h in order], 5 * heads)
    norm = rows_ref[0:heads, :]
    cum = rows_ref[heads : 2 * heads, :]
    beta = rows_ref[4 * heads : 5 * heads, :]
    inverse = 1.0 / jnp.maximum(jnp.sqrt(norm), rows_ref[5 * heads : 6 * heads, :])
    last = cum[:, n - 1 : n]
    carry = inverse * jnp.exp(last - cum)
    lift = jnp.exp(last)
    rows_ref[6 * heads : 7 * heads, :] = beta * inverse
    rows_ref[7 * heads : 8 * heads, :] = carry
    columns = rows_ref[...].T

    def column(kind, item):
        at = kind * heads + item
        return columns[:, at : at + 1]

    systems, inverses = [], []
    for item in range(heads):
        spread = column(1, item) - cum[item : item + 1, :]
        damping = jnp.exp(jnp.where(row > col, spread, 0.0))
        system = jnp.where(
            row > col,
            grams[item] * damping * column(6, item) * inverse[item : item + 1, :],
            0.0,
        )
        systems.append(split(system))
        inverses.append(
            jnp.where(row == col, 1.0, jnp.where((row ^ col) == 1, -system, 0.0))
        )
    size = 2
    while size < n:
        joins = ((row ^ col) & ~(2 * size - 1)) == 0
        joins = joins & ((row & size) != 0) & ((col & size) == 0)
        parts = [split(x) for x in inverses]
        mids = [split(dot_square(a, x)) for a, x in zip(systems, parts)]
        ends = [dot_square(x, t) for x, t in zip(parts, mids)]
        inverses = [x - jnp.where(joins, e, 0.0) for x, e in zip(inverses, ends)]
        size *= 2

    flat_ref[...] = value_ref[...].astype(F32)
    write_scale = beta * jnp.exp(cum) * inverse
    for item, head in enumerate(order):
        x = inverses[item]
        value = flat_ref[pl.ds(head, n, stride=heads), :].astype(BF16)
        key = keys[item]
        w = mm(
            jnp.concatenate(split(x * write_scale[item : item + 1, :]), 1),
            jnp.concatenate([key, key], 0),
        )
        u = mm(
            jnp.concatenate(split(x * beta[item : item + 1, :]), 1),
            jnp.concatenate([value, value], 0),
        )
        wu = jnp.concatenate([w, u], 1)
        wu_ref[item] = wu
        scaled = split(wu * column(7, item))
        both = mm(
            jnp.concatenate([keys_t[item], keys_t[item]], 1), jnp.concatenate(scaled, 0)
        )
        ends = jnp.where(row == col, lift[item : item + 1, :], 0.0)
        maps_refs[item // per][item % per] = jnp.concatenate([ends - both[:, :d], both[:, d:]], 1)


def output_kernel(
    groups,
    per,
    tokens_all,
    rank_ref,
    query_ref,
    key_ref,
    total_ref,
    cum_ref,
    wu_ref,
    left_ref,
    right_ref,
    flat_ref,
    rows_ref,
):
    heads = groups * per
    n = cum_ref.shape[1]
    d = key_ref.shape[1]
    blocks = n // BLOCK
    order = item_heads(rank_ref, groups, per)
    row, col = iotas(n, n)
    limit = jnp.sqrt(jnp.sum(total_ref[...], 1, keepdims=True) / tokens_all + EPSILON)
    rows_ref[0:heads, :] = jnp.broadcast_to(limit, (heads, n))
    gather_rows(rows_ref, rows_ref, order, heads)
    gather_rows(cum_ref, rows_ref, order, 2 * heads)
    limit = rows_ref[heads : 2 * heads, :]
    cum = rows_ref[2 * heads : 3 * heads, :]
    flat_ref[...] = key_ref[...].astype(F32)
    keys = [flat_ref[pl.ds(head, n, stride=heads), :] for head in order]
    flat_ref[...] = query_ref[...].astype(F32)
    queries = [flat_ref[pl.ds(head, n, stride=heads), :] for head in order]
    norms = []
    for item in range(heads):
        norms.append(jnp.sum(keys[item] * keys[item], 1, keepdims=True))
    position = lax.broadcasted_iota(jnp.int32, (heads, n), 1)
    kinds = [cum]
    for b in range(1, blocks):
        end = b * BLOCK
        kinds.append(
            jnp.where(position < end, jnp.exp(jnp.minimum(cum[:, end - 1 : end] - cum, 0.0)), 0.0)
        )
    kinds.append(limit)
    for at, kind in enumerate(kinds):
        rows_ref[at * heads : (at + 1) * heads, :] = kind
    columns = rows_ref[...].T
    spare = len(kinds) * heads
    inverse_columns = [
        1.0
        / jnp.maximum(
            jnp.sqrt(norms[item]),
            columns[:, (len(kinds) - 1) * heads + item : (len(kinds) - 1) * heads + item + 1],
        )
        for item in range(heads)
    ]
    for item in range(heads):
        wu = wu_ref[item]
        key = keys[item].astype(BF16)
        key_t = key.T
        query = queries[item]
        cum_column = columns[:, item : item + 1]
        inverse = inverse_columns[item]
        reach = (
            1.0
            / jnp.sqrt(jnp.sum(query * query, 1, keepdims=True) + EPSILON)
            * (d**-0.5)
        )
        scores = mm(query.astype(BF16), key_t)
        spread = jnp.where(row >= col, cum_column - cum[item : item + 1, :], 0.0)
        scores = jnp.where(row >= col, scores * jnp.exp(spread), 0.0) * reach
        scaled = split(wu * inverse)
        both = dot_split(split(scores), scaled)
        rest = [query * (reach * jnp.exp(cum_column)) - both[:, :d]]
        outs = [both[:, d:]]
        for b in range(1, blocks):
            carry = columns[:, b * heads + item : b * heads + item + 1]
            part = split(wu * (inverse * carry))
            inner = mm(jnp.concatenate([key_t, key_t], 1), jnp.concatenate(part, 0))
            at = b * BLOCK - 1
            ends = jnp.where(row == col, jnp.exp(cum[item : item + 1, at : at + 1]), 0.0)
            rest.append(ends - inner[:, :d])
            outs.append(inner[:, d:])
        left_ref[item] = jnp.concatenate(split(jnp.concatenate(rest, 0)), 1)
        right_ref[item] = jnp.concatenate(outs, 0)


def join(latter, earlier):
    d = latter.shape[0]
    both = dot_split(split(latter[:, :d]), split(earlier))
    return jnp.concatenate([both[:, :d], both[:, d:] + latter[:, d:]], 1)


def apply(step, state):
    d = state.shape[0]
    return dot_split(split(step[:, :d]), split(state)) + step[:, d:]


def compose_kernel(groups, per, rank_ref, *refs):
    parts, (prefix_ref, total_ref, held_ref) = refs[:groups], refs[groups:]
    for slot in range(groups):
        held_ref[slot ^ rank_ref[0]] = parts[slot][...]
    so_far = [held_ref[0, i] for i in range(per)]
    for place in range(1, groups):
        for i in range(per):
            prefix_ref[place - 1, i] = so_far[i]
        so_far = [join(held_ref[place, i], so_far[i]) for i in range(per)]
    for i in range(per):
        total_ref[i] = so_far[i]


def middle_kernel(per, upper_ref, mine_ref, other_ref, start_ref, state_ref):
    for i in range(per):
        mine, other = mine_ref[i], other_ref[i]
        upper = upper_ref[0] != 0
        earlier = jnp.where(upper, other, mine)
        latter = jnp.where(upper, mine, other)
        state_ref[i] = apply(latter, apply(earlier, start_ref[i]))


def enter_kernel(
    groups, per, rank_ref, upper_ref, later_ref, prefix_ref, before_ref, start_ref, came_ref, *refs
):
    out_refs, out_ref = refs[:groups], refs[groups]
    for i in range(per):
        state = jnp.where(later_ref[0] != 0, came_ref[i], start_ref[i])
        moved = apply(before_ref[i], state)
        state = jnp.where(upper_ref[0] != 0, moved, state)
        out_ref[rank_ref[0], i] = state
        for place in range(1, groups):
            out_ref[place ^ rank_ref[0], i] = apply(prefix_ref[place - 1, i], state)
    for slot in range(groups):
        out_refs[slot][...] = out_ref[slot]


def finish_kernel(groups, per, rank_ref, *refs):
    states = refs[:groups]
    left_ref, right_ref, gate_ref, out_ref, block_ref, flat_ref, gates_ref = refs[groups:]
    heads = groups * per
    order = item_heads(rank_ref, groups, per)
    d = gate_ref.shape[1]
    n = gate_ref.shape[0] // heads
    blocks = block_ref.shape[0]
    gates_ref[...] = gate_ref[...].astype(F32)
    for item, head in enumerate(order):
        state = states[item // per][item % per]
        high, low = split(state)
        left = left_ref[item]
        both = mm(left, jnp.concatenate([high, high], 0)) + mm(left[:, :d], low) + right_ref[item]
        raw = both[:n]
        block_ref[0, head] = state
        for b in range(1, blocks):
            block_ref[b, head] = both[n + (b - 1) * d : n + b * d]
        gate = gates_ref[pl.ds(head, n, stride=heads), :]
        scale = 1.0 / jnp.sqrt(jnp.mean(raw * raw, 1, keepdims=True) + EPSILON)
        flat_ref[pl.ds(head, n, stride=heads), :] = raw * scale * (gate / (1.0 + jnp.exp(-gate)))
    out_ref[...] = flat_ref[...].astype(BF16)


def exact(matrix, operand):
    return jnp.einsum("...ij,...jk->...ik", matrix, operand, precision=lax.Precision.HIGHEST)


def chain(latter, earlier):
    d = latter.shape[-2]
    both = exact(latter[..., :d], earlier)
    return jnp.concatenate([both[..., :d], both[..., d:] + latter[..., d:]], -1)


def flag(value):
    return jnp.reshape(value, (1,)).astype(jnp.int32)


def on_device(
    queries, key_vectors, values, out_gate, inputs, beta_weight, log_decay, initial_state
):
    n, heads, d = queries.shape
    blocks = n // BLOCK
    count, place = lax.axis_size("seq"), lax.axis_index("seq")
    groups = math.gcd(math.gcd(4, heads), count)
    per = heads // groups
    runs = count // groups
    rounds = runs.bit_length() - 1
    assert runs == 1 << rounds
    rank = flag(place % groups)
    run = place // groups

    def flipped(mask):
        return [(i, i ^ mask) for i in range(count)]

    def flat(tensor):
        return tensor.reshape(n * heads, d)

    total, logits = call(
        functools.partial(stats_kernel, heads),
        (shape(heads, d), shape(beta_weight.shape[0], n)),
        operands=3,
        name="stats",
    )(flat(key_vectors), beta_weight, inputs)
    if lax.axis_size("head") == 2:
        side = lax.axis_index("head")
        halves = logits.reshape(2, heads, n)
        own = lax.dynamic_index_in_dim(halves, side, 0, keepdims=False)
        theirs = lax.dynamic_index_in_dim(halves, 1 - side, 0, keepdims=False)
        logits = own + lax.ppermute(theirs, "head", [(0, 1), (1, 0)])
    else:
        logits = lax.psum_scatter(logits, "head", scatter_dimension=0, tiled=True)
    mask = 1
    while mask < count:
        total = total + lax.ppermute(total, "seq", flipped(mask))
        mask *= 2

    tokens_all = n * count
    *maps, wu, cum = call(
        functools.partial(solve_kernel, groups, per, tokens_all),
        [shape(per, d, 2 * d)] * groups + [shape(heads, n, 2 * d), shape(heads, n)],
        scratch=(pltpu.VMEM((n * heads, d), F32), pltpu.VMEM((128, n), F32)),
        scalars=1,
        operands=5,
        flops=1 << 30,
        name="solve",
    )(rank, flat(key_vectors), flat(values), logits, total, log_decay)

    parts = [maps[0]] + [
        lax.ppermute(maps[slot], "seq", flipped(slot)) for slot in range(1, groups)
    ]
    left, right = call(
        functools.partial(output_kernel, groups, per, tokens_all),
        (shape(heads, n + (blocks - 1) * d, 2 * d, dtype=BF16), shape(heads, n + (blocks - 1) * d, d)),
        scratch=(pltpu.VMEM((n * heads, d), F32), pltpu.VMEM((128, n), F32)),
        scalars=1,
        operands=5,
        flops=1 << 30,
        name="outputs",
    )(rank, flat(queries), flat(key_vectors), total, cum, wu)

    prefix, run_map = call(
        functools.partial(compose_kernel, groups, per),
        (shape(max(groups - 1, 1), per, d, 2 * d), shape(per, d, 2 * d)),
        scratch=(pltpu.VMEM((groups, per, d, 2 * d), F32),),
        scalars=1,
        operands=groups,
        flops=1 << 27,
        name="compose",
    )(rank, *parts)
    start = lax.dynamic_slice_in_dim(initial_state, (place % groups) * per, per, 0)

    before, upper, came, later = run_map, flag(0), start, flag(0)
    if rounds == 2:
        other = lax.ppermute(run_map, "seq", flipped(groups))
        upper = flag(run & 1)
        before = other
        middle = call(
            functools.partial(middle_kernel, per),
            shape(per, d, d),
            scalars=1,
            operands=3,
            name="middle",
        )(upper, run_map, other, start)
    elif rounds:
        eye = jnp.broadcast_to(jnp.eye(d, 2 * d, dtype=F32), run_map.shape)
        before, upper, window = eye, flag(1), run_map
        for r in range(rounds - 1):
            other = lax.ppermute(window, "seq", flipped(groups << r))
            high = (run >> r) & 1 == 1
            before = jnp.where(high, chain(before, other), before)
            window = chain(jnp.where(high, window, other), jnp.where(high, other, window))
        middle = exact(window[..., :d], start) + window[..., d:]
    if rounds:
        half = count // 2
        came = lax.ppermute(middle, "seq", [(i, i + half) for i in range(half)])
        later = flag(run >= runs // 2)
    entries = call(
        functools.partial(enter_kernel, groups, per),
        [shape(per, d, d)] * groups,
        scratch=(pltpu.VMEM((groups, per, d, d), F32),),
        scalars=3,
        operands=4,
        flops=1 << 27,
        name="enter",
    )(rank, upper, later, prefix, before, start, came)

    states = [entries[0]] + [
        lax.ppermute(entries[slot], "seq", flipped(slot)) for slot in range(1, groups)
    ]
    gated, block_states = call(
        functools.partial(finish_kernel, groups, per),
        (shape(n * heads, d, dtype=BF16), shape(blocks, heads, d, d)),
        scratch=(pltpu.VMEM((n * heads, d), F32), pltpu.VMEM((n * heads, d), F32)),
        scalars=1,
        operands=groups + 3,
        flops=1 << 28,
        name="finish",
    )(rank, *states, left, right, flat(out_gate))
    return (gated.reshape(n, heads, d), block_states)


def solution(mesh):
    return jax.shard_map(
        on_device,
        mesh=mesh,
        in_specs=(
            P("seq", "head", None),
            P("seq", "head", None),
            P("seq", "head", None),
            P("seq", "head", None),
            P("seq", "head"),
            P(None, "head"),
            P("head", "seq"),
            P("head", None, None),
        ),
        out_specs=(P("seq", "head", None), P("seq", "head", None, None)),
        check_vma=False,
    )
```

```python
import functools
import math

import jax
import jax.numpy as jnp
from jax import lax
from jax.experimental import pallas as pl
from jax.experimental.pallas import tpu as pltpu
from jax.sharding import PartitionSpec as P


BLOCK = 64
EPSILON = 1e-06
F32 = jnp.float32
BF16 = jnp.bfloat16
VMEM_LIMIT = 20 * 1024 * 1024


def split(x):
    high = x.astype(BF16)
    return high, (x - high.astype(F32)).astype(BF16)


def mm(a, b):
    return jnp.dot(a, b, preferred_element_type=F32)


def dot_split(left, right):
    (lh, ll), (rh, rl) = left, right
    return mm(jnp.concatenate([lh, ll], 1), jnp.concatenate([rh, rh], 0)) + mm(lh, rl)


def dot_square(left, right):
    (lh, ll), (rh, rl) = left, right
    n = rh.shape[1]
    wide = mm(
        jnp.concatenate([lh, ll], 1),
        jnp.concatenate(
            [jnp.concatenate([rh, rl], 1), jnp.concatenate([rh, jnp.zeros_like(rl)], 1)], 0
        ),
    )
    return wide[:, :n] + wide[:, n:]


def iotas(n, m):
    return (
        lax.broadcasted_iota(jnp.int32, (n, m), 0),
        lax.broadcasted_iota(jnp.int32, (n, m), 1),
    )


def vmem(count):
    return [pl.BlockSpec(memory_space=pltpu.VMEM)] * count


def smem():
    return pl.BlockSpec(memory_space=pltpu.SMEM)


def call(kernel, out_shape, scratch=(), scalars=0, operands=0, anywhere=0, flops=0, grant=VMEM_LIMIT):
    single = not isinstance(out_shape, (list, tuple))
    return pl.pallas_call(
        kernel,
        out_shape=out_shape,
        in_specs=[smem()] * scalars
        + [pl.BlockSpec(memory_space=pltpu.HBM)] * anywhere
        + vmem(operands),
        out_specs=vmem(1)[0] if single else vmem(len(out_shape)),
        scratch_shapes=list(scratch),
        compiler_params=pltpu.CompilerParams(vmem_limit_bytes=grant),
        cost_estimate=pl.CostEstimate(flops=flops, bytes_accessed=1 << 20, transcendentals=0),
    )


def shape(*dims, dtype=F32):
    return jax.ShapeDtypeStruct(dims, dtype)


def norms_kernel(heads, key_ref, total_ref):
    keys = key_ref[...].astype(F32)
    squares = keys * keys
    rows = squares.shape[0]
    total_ref[...] = squares.reshape(rows // heads, heads, squares.shape[1]).sum(0)


def logits_kernel(heads, pair, side_ref, weight_ref, inputs_ref, *refs):
    logits = lax.dot_general(
        weight_ref[...], inputs_ref[...], (((1,), (1,)), ((), ())), preferred_element_type=F32
    )
    if pair:
        own_ref, theirs_ref, full_ref = refs
        full_ref[...] = logits
        mine = pl.multiple_of(side_ref[0] * heads, heads)
        own_ref[...] = full_ref[pl.ds(mine, heads), :]
        theirs_ref[...] = full_ref[pl.ds(heads - mine, heads), :]
    else:
        refs[0][...] = logits


def pack_kernel(
    groups, per, rank_ref, key_ref, value_ref, decay_ref, own_ref, came_ref, *refs
):
    out_refs, (flat_ref, logit_ref) = refs[:groups], refs[groups:]
    heads, n = decay_ref.shape
    logit_ref[...] = own_ref[...] + came_ref[...]
    for at, source in enumerate((key_ref, value_ref)):
        flat_ref[...] = source[...].astype(F32)
        for slot in range(groups):
            for i in range(per):
                head = (slot ^ rank_ref[0]) * per + i
                out_refs[slot][i, at * n : (at + 1) * n] = flat_ref[
                    pl.ds(head, n, stride=heads), :
                ]
    for slot in range(groups):
        for i in range(per):
            head = (slot ^ rank_ref[0]) * per + i
            out_refs[slot][i, 2 * n : 2 * n + 1] = decay_ref[pl.ds(head, 1), :]
            out_refs[slot][i, 2 * n + 1 : 2 * n + 2] = logit_ref[pl.ds(head, 1), :]
            out_refs[slot][i, 2 * n + 2 :] = jnp.zeros((6, n), F32)


def sums_along(decay):
    lane = lax.broadcasted_iota(jnp.int32, decay.shape, 1)
    step = 1
    while step < decay.shape[1]:
        decay = decay + jnp.where(lane >= step, pltpu.roll(decay, step, 1), 0.0)
        step *= 2
    return decay


def limits(total, tokens_all):
    return jnp.sqrt(jnp.sum(total, 1, keepdims=True) / tokens_all + EPSILON)


def solve(keys, values, decay, logits, limit, rows_ref):
    items, n = decay.shape
    row, col = iotas(n, n)
    cum = sums_along(decay)
    beta = 1.0 / (1.0 + jnp.exp(-logits))
    keys_t = [key.T for key in keys]
    grams = [mm(key, key_t) for key, key_t in zip(keys, keys_t)]
    norm = jnp.concatenate(
        [jnp.sum(jnp.where(row == col, gram, 0.0), 0, keepdims=True) for gram in grams], 0
    )
    inverse = 1.0 / jnp.maximum(jnp.sqrt(norm), limit)
    for at, kind in enumerate((cum, beta * inverse, inverse)):
        rows_ref[at * items : (at + 1) * items, :] = kind
    columns = rows_ref[...].T

    def column(kind, item):
        at = kind * items + item
        return columns[:, at : at + 1]

    systems, inverses = [], []
    for item in range(items):
        spread = column(0, item) - cum[item : item + 1, :]
        damping = jnp.exp(jnp.where(row > col, spread, 0.0))
        system = jnp.where(
            row > col,
            grams[item] * damping * column(1, item) * inverse[item : item + 1, :],
            0.0,
        )
        systems.append(split(system))
        inverses.append(
            jnp.where(row == col, 1.0, jnp.where((row ^ col) == 1, -system, 0.0))
        )
    size = 2
    while size < n:
        joins = ((row ^ col) & ~(2 * size - 1)) == 0
        joins = joins & ((row & size) != 0) & ((col & size) == 0)
        parts = [split(x) for x in inverses]
        mids = [split(dot_square(a, x)) for a, x in zip(systems, parts)]
        ends = [dot_square(x, t) for x, t in zip(parts, mids)]
        inverses = [x - jnp.where(joins, e, 0.0) for x, e in zip(inverses, ends)]
        size *= 2
    write_scale = beta * jnp.exp(cum) * inverse
    writes = []
    for item in range(items):
        x, key, value = inverses[item], keys[item], values[item]
        w = mm(
            jnp.concatenate(split(x * write_scale[item : item + 1, :]), 1),
            jnp.concatenate([key, key], 0),
        )
        u = mm(
            jnp.concatenate(split(x * beta[item : item + 1, :]), 1),
            jnp.concatenate([value, value], 0),
        )
        writes.append(jnp.concatenate([w, u], 1) * column(2, item))
    return writes, keys_t, cum, [column(0, item) for item in range(items)]


def read_map(write, key_t, carry, lift, row, col):
    d = key_t.shape[0]
    both = mm(
        jnp.concatenate([key_t, key_t], 1), jnp.concatenate(split(write * carry), 0)
    )
    ends = jnp.where(row == col, lift, 0.0)
    return jnp.concatenate([ends - both[:, :d], both[:, d:]], 1)


def run_kernel(groups, per, tokens_all, rank_ref, total_ref, *refs):
    packs, (prefix_ref, run_ref, rows_ref, held_ref) = refs[:groups], refs[groups:]
    n = total_ref.shape[1]
    row, col = iotas(n, n)
    items = [(slot, i) for slot in range(groups) for i in range(per)]
    limit = limits(total_ref[...], tokens_all)
    rows_ref[0 : limit.shape[0], :] = jnp.broadcast_to(limit, (limit.shape[0], n))
    limit = jnp.concatenate(
        [rows_ref[pl.ds(rank_ref[0] * per + i, 1), :] for _, i in items], 0
    )
    keys = [packs[slot][i, 0:n].astype(BF16) for slot, i in items]
    values = [packs[slot][i, n : 2 * n].astype(BF16) for slot, i in items]
    decay = jnp.concatenate([packs[slot][i, 2 * n : 2 * n + 1] for slot, i in items], 0)
    logits = jnp.concatenate([packs[slot][i, 2 * n + 1 : 2 * n + 2] for slot, i in items], 0)
    writes, keys_t, cum, cum_columns = solve(keys, values, decay, logits, limit, rows_ref)
    for item, (slot, i) in enumerate(items):
        last = cum[item : item + 1, n - 1 : n]
        held_ref[slot ^ rank_ref[0], i] = read_map(
            writes[item], keys_t[item], jnp.exp(last - cum_columns[item]), jnp.exp(last), row, col
        )
    so_far = [held_ref[0, i] for i in range(per)]
    for place in range(1, groups):
        for i in range(per):
            prefix_ref[place - 1, i] = so_far[i]
        so_far = [join(held_ref[place, i], so_far[i]) for i in range(per)]
    for i in range(per):
        run_ref[i] = so_far[i]


def own_kernel(
    tokens_all,
    key_ref,
    value_ref,
    own_ref,
    came_ref,
    total_ref,
    decay_ref,
    wu_ref,
    cum_ref,
    flat_ref,
    rows_ref,
):
    heads, n = decay_ref.shape
    flat_ref[...] = key_ref[...].astype(F32)
    keys = [flat_ref[pl.ds(h, n, stride=heads), :].astype(BF16) for h in range(heads)]
    flat_ref[...] = value_ref[...].astype(F32)
    values = [flat_ref[pl.ds(h, n, stride=heads), :].astype(BF16) for h in range(heads)]
    writes, _, cum, _ = solve(
        keys,
        values,
        decay_ref[...],
        own_ref[...] + came_ref[...],
        limits(total_ref[...], tokens_all),
        rows_ref,
    )
    cum_ref[...] = cum
    for h in range(heads):
        wu_ref[h] = writes[h]


def output_kernel(
    query_ref, key_ref, cum_ref, wu_ref, left_ref, right_ref, flat_ref, rows_ref
):
    heads, n = cum_ref.shape
    d = key_ref.shape[1]
    blocks = n // BLOCK
    row, col = iotas(n, n)
    cum = cum_ref[...]
    flat_ref[...] = key_ref[...].astype(F32)
    keys = [flat_ref[pl.ds(h, n, stride=heads), :].astype(BF16) for h in range(heads)]
    flat_ref[...] = query_ref[...].astype(F32)
    queries = [flat_ref[pl.ds(h, n, stride=heads), :] for h in range(heads)]
    position = lax.broadcasted_iota(jnp.int32, (heads, n), 1)
    kinds = [cum]
    for b in range(1, blocks):
        end = b * BLOCK
        fall = jnp.exp(jnp.minimum(cum[:, end - 1 : end] - cum, 0.0))
        kinds.append(jnp.where(position < end, fall, 0.0))
    for at, kind in enumerate(kinds):
        rows_ref[at * heads : (at + 1) * heads, :] = kind
    columns = rows_ref[...].T
    for h in range(heads):
        write, key_t, query = wu_ref[h], keys[h].T, queries[h]
        cum_column = columns[:, h : h + 1]
        reach = (
            1.0 / jnp.sqrt(jnp.sum(query * query, 1, keepdims=True) + EPSILON) * (d**-0.5)
        )
        scores = mm(query.astype(BF16), key_t)
        spread = jnp.where(row >= col, cum_column - cum[h : h + 1, :], 0.0)
        scores = jnp.where(row >= col, scores * jnp.exp(spread), 0.0) * reach
        both = dot_split(split(scores), split(write))
        rest = [query * (reach * jnp.exp(cum_column)) - both[:, :d]]
        outs = [both[:, d:]]
        for b in range(1, blocks):
            at = b * BLOCK - 1
            carry = columns[:, b * heads + h : b * heads + h + 1]
            inner = read_map(
                write, key_t, carry, jnp.exp(cum[h : h + 1, at : at + 1]), row, col
            )
            rest.append(inner[:, :d])
            outs.append(inner[:, d:])
        left_ref[h] = jnp.concatenate(split(jnp.concatenate(rest, 0)), 1)
        right_ref[h] = jnp.concatenate(outs, 0)


def join(latter, earlier):
    d = latter.shape[0]
    both = dot_split(split(latter[:, :d]), split(earlier))
    return jnp.concatenate([both[:, :d], both[:, d:] + latter[:, d:]], 1)


def apply(step, state):
    d = state.shape[0]
    return dot_split(split(step[:, :d]), split(state)) + step[:, d:]


def middle_kernel(per, upper_ref, mine_ref, other_ref, start_ref, state_ref):
    for i in range(per):
        mine, other = mine_ref[i], other_ref[i]
        upper = upper_ref[0] != 0
        earlier = jnp.where(upper, other, mine)
        latter = jnp.where(upper, mine, other)
        state_ref[i] = apply(latter, apply(earlier, start_ref[i]))


def enter_kernel(
    groups, per, rank_ref, upper_ref, later_ref, prefix_ref, before_ref, start_ref, came_ref, *refs
):
    out_refs, out_ref = refs[:groups], refs[groups]
    for i in range(per):
        state = jnp.where(later_ref[0] != 0, came_ref[i], start_ref[i])
        moved = apply(before_ref[i], state)
        state = jnp.where(upper_ref[0] != 0, moved, state)
        out_ref[rank_ref[0], i] = state
        for place in range(1, groups):
            out_ref[place ^ rank_ref[0], i] = apply(prefix_ref[place - 1, i], state)
    for slot in range(groups):
        out_refs[slot][...] = out_ref[slot]


def finish_kernel(groups, per, rank_ref, *refs):
    states = refs[:groups]
    left_ref, right_ref, gate_ref, out_ref, block_ref, flat_ref, gates_ref = refs[groups:]
    heads = groups * per
    order = [(slot ^ rank_ref[0]) * per + i for slot in range(groups) for i in range(per)]
    d = gate_ref.shape[1]
    n = gate_ref.shape[0] // heads
    blocks = block_ref.shape[0]
    gates_ref[...] = gate_ref[...].astype(F32)
    for item, head in enumerate(order):
        state = states[item // per][item % per]
        high, low = split(state)
        left = left_ref[head]
        both = mm(left, jnp.concatenate([high, high], 0)) + mm(left[:, :d], low) + right_ref[head]
        raw = both[:n]
        block_ref[0, head] = state
        for b in range(1, blocks):
            block_ref[b, head] = both[n + (b - 1) * d : n + b * d]
        gate = gates_ref[pl.ds(head, n, stride=heads), :]
        scale = 1.0 / jnp.sqrt(jnp.mean(raw * raw, 1, keepdims=True) + EPSILON)
        flat_ref[pl.ds(head, n, stride=heads), :] = raw * scale * (gate / (1.0 + jnp.exp(-gate)))
    out_ref[...] = flat_ref[...].astype(BF16)


def exact(matrix, operand):
    return jnp.einsum("...ij,...jk->...ik", matrix, operand, precision=lax.Precision.HIGHEST)


def chain(latter, earlier):
    d = latter.shape[-2]
    both = exact(latter[..., :d], earlier)
    return jnp.concatenate([both[..., :d], both[..., d:] + latter[..., d:]], -1)


def flag(value):
    return jnp.reshape(value, (1,)).astype(jnp.int32)


def on_device(
    queries, key_vectors, values, out_gate, inputs, beta_weight, log_decay, initial_state
):
    n, heads, d = queries.shape
    blocks = n // BLOCK
    count, place = lax.axis_size("seq"), lax.axis_index("seq")
    groups = math.gcd(math.gcd(4, heads), count)
    per = heads // groups
    runs = count // groups
    rounds = runs.bit_length() - 1
    assert runs == 1 << rounds
    rank = flag(place % groups)
    run = place // groups

    def flipped(mask):
        return [(i, i ^ mask) for i in range(count)]

    def flat(tensor):
        return tensor.reshape(n * heads, d)

    pair = lax.axis_size("head") == 2
    all_heads = beta_weight.shape[0]
    total = call(
        functools.partial(norms_kernel, heads), shape(heads, d), operands=1, flops=1 << 31
    )(flat(key_vectors))
    logits = call(
        functools.partial(logits_kernel, heads, pair),
        [shape(heads, n)] * 2 if pair else [shape(all_heads, n)],
        scratch=(pltpu.VMEM((all_heads, n), F32),) if pair else (),
        scalars=1,
        operands=2,
        flops=1 << 24,
    )(flag(lax.axis_index("head")), beta_weight, inputs)
    if pair:
        own, theirs = logits
        came = lax.ppermute(theirs, "head", [(0, 1), (1, 0)])
    else:
        own = lax.psum_scatter(logits[0], "head", scatter_dimension=0, tiled=True)
        came = jnp.zeros_like(own)
    packs = call(
        functools.partial(pack_kernel, groups, per),
        [shape(per, 2 * n + 8, d)] * groups,
        scratch=(pltpu.VMEM((n * heads, d), F32), pltpu.VMEM((heads, n), F32)),
        scalars=1,
        operands=5,
        flops=1 << 24,
    )(rank, flat(key_vectors), flat(values), log_decay, own, came)

    def summed(total, mask):
        return total + lax.ppermute(total, "seq", flipped(mask))

    for slot in range(1, groups):
        if slot & (slot - 1) == 0:
            total = summed(total, slot)
            if slot == 1:
                total, packs = lax.optimization_barrier((total, packs))
    exchanged = []
    for slot in range(1, groups):
        exchanged.append(lax.ppermute(packs[slot], "seq", flipped(slot)))
    packs = [packs[0]] + exchanged
    mask = groups
    while mask < count:
        total = summed(total, mask)
        mask *= 2

    tokens_all = n * count
    prefix, run_map = call(
        functools.partial(run_kernel, groups, per, tokens_all),
        (shape(max(groups - 1, 1), per, d, 2 * d), shape(per, d, 2 * d)),
        scratch=(pltpu.VMEM((128, n), F32), pltpu.VMEM((groups, per, d, 2 * d), F32)),
        scalars=1,
        operands=1 + groups,
        flops=1 << 30,
    )(rank, total, *packs)

    wu, cum = call(
        functools.partial(own_kernel, tokens_all),
        (shape(heads, n, 2 * d), shape(heads, n)),
        scratch=(pltpu.VMEM((n * heads, d), F32), pltpu.VMEM((128, n), F32)),
        operands=6,
        flops=1 << 31,
    )(flat(key_vectors), flat(values), own, came, total, log_decay)
    start = lax.dynamic_slice_in_dim(initial_state, (place % groups) * per, per, 0)

    before, upper, came, later = run_map, flag(0), start, flag(0)
    if rounds == 2:
        other = lax.ppermute(run_map, "seq", flipped(groups))
        other, wu = lax.optimization_barrier((other, wu))
        upper = flag(run & 1)
        before = other
        middle = call(
            functools.partial(middle_kernel, per), shape(per, d, d), scalars=1, operands=3
        )(upper, run_map, other, start)
    elif rounds:
        eye = jnp.broadcast_to(jnp.eye(d, 2 * d, dtype=F32), run_map.shape)
        before, upper, window = eye, flag(1), run_map
        for r in range(rounds - 1):
            other = lax.ppermute(window, "seq", flipped(groups << r))
            high = (run >> r) & 1 == 1
            before = jnp.where(high, chain(before, other), before)
            window = chain(jnp.where(high, window, other), jnp.where(high, other, window))
        middle = exact(window[..., :d], start) + window[..., d:]
    if rounds:
        mirror = [(i, (runs - 1 - i // groups) * groups + i % groups) for i in range(count)]
        came = lax.ppermute(middle, "seq", mirror)
        later = flag(run >= runs // 2)
    rows = n + (blocks - 1) * d
    left, right = call(
        output_kernel,
        (shape(heads, rows, 2 * d, dtype=BF16), shape(heads, rows, d)),
        scratch=(pltpu.VMEM((n * heads, d), F32), pltpu.VMEM((128, n), F32)),
        operands=4,
        flops=1 << 30,
    )(flat(queries), flat(key_vectors), cum, wu)
    came, left = lax.optimization_barrier((came, left))
    entries = call(
        functools.partial(enter_kernel, groups, per),
        [shape(per, d, d)] * groups,
        scratch=(pltpu.VMEM((groups, per, d, d), F32),),
        scalars=3,
        operands=4,
        flops=1 << 27,
    )(rank, upper, later, prefix, before, start, came)

    states = [entries[0]] + [
        lax.ppermute(entries[slot], "seq", flipped(slot)) for slot in range(1, groups)
    ]
    gated, block_states = call(
        functools.partial(finish_kernel, groups, per),
        (shape(n * heads, d, dtype=BF16), shape(blocks, heads, d, d)),
        scratch=(pltpu.VMEM((n * heads, d), F32), pltpu.VMEM((n * heads, d), F32)),
        scalars=1,
        operands=groups + 3,
        flops=1 << 28,
    )(rank, *states, left, right, flat(out_gate))
    return (gated.reshape(n, heads, d), block_states)


def solution(mesh):
    return jax.shard_map(
        on_device,
        mesh=mesh,
        in_specs=(
            P("seq", "head", None),
            P("seq", "head", None),
            P("seq", "head", None),
            P("seq", "head", None),
            P("seq", "head"),
            P(None, "head"),
            P("head", "seq"),
            P("head", None, None),
        ),
        out_specs=(P("seq", "head", None), P("seq", "head", None, None)),
        check_vma=False,
    )
```

```python
import functools
import math

import jax
import jax.numpy as jnp
from jax import lax
from jax.experimental import pallas as pl
from jax.experimental.pallas import tpu as pltpu
from jax.sharding import PartitionSpec as P


BLOCK = 64
EPSILON = 1e-06
F32 = jnp.float32
BF16 = jnp.bfloat16
VMEM_LIMIT = 20 * 1024 * 1024


def split(x):
    high = x.astype(BF16)
    return high, (x - high.astype(F32)).astype(BF16)


def mm(a, b):
    return jnp.dot(a, b, preferred_element_type=F32)


def dot_split(left, right):
    (lh, ll), (rh, rl) = left, right
    return mm(jnp.concatenate([lh, ll], 1), jnp.concatenate([rh, rh], 0)) + mm(lh, rl)


def dot_square(left, right):
    (lh, ll), (rh, rl) = left, right
    n = rh.shape[1]
    wide = mm(
        jnp.concatenate([lh, ll], 1),
        jnp.concatenate(
            [jnp.concatenate([rh, rl], 1), jnp.concatenate([rh, jnp.zeros_like(rl)], 1)], 0
        ),
    )
    return wide[:, :n] + wide[:, n:]


def iotas(n, m):
    return (
        lax.broadcasted_iota(jnp.int32, (n, m), 0),
        lax.broadcasted_iota(jnp.int32, (n, m), 1),
    )


def vmem(count):
    return [pl.BlockSpec(memory_space=pltpu.VMEM)] * count


def smem():
    return pl.BlockSpec(memory_space=pltpu.SMEM)


def call(kernel, out_shape, scratch=(), scalars=0, operands=0, anywhere=0, flops=0, grant=VMEM_LIMIT):
    single = not isinstance(out_shape, (list, tuple))
    return pl.pallas_call(
        kernel,
        out_shape=out_shape,
        in_specs=[smem()] * scalars
        + [pl.BlockSpec(memory_space=pltpu.HBM)] * anywhere
        + vmem(operands),
        out_specs=vmem(1)[0] if single else vmem(len(out_shape)),
        scratch_shapes=list(scratch),
        compiler_params=pltpu.CompilerParams(vmem_limit_bytes=grant),
        cost_estimate=pl.CostEstimate(flops=flops, bytes_accessed=1 << 20, transcendentals=0),
    )


def shape(*dims, dtype=F32):
    return jax.ShapeDtypeStruct(dims, dtype)


def zeros_kernel(out_ref):
    out_ref[...] = jnp.zeros_like(out_ref)


def stats_kernel(
    heads, pair, side_ref, zeros_ref, key_ref, weight_ref, inputs_ref, decay_ref, total_ref, cum_ref, *refs
):
    logits = lax.dot_general(
        weight_ref[...], inputs_ref[...], (((1,), (1,)), ((), ())), preferred_element_type=F32
    )
    if pair:
        own_ref, theirs_ref, full_ref = refs
        full_ref[...] = logits
        mine = pl.multiple_of(side_ref[0] * heads, heads)
        own_ref[...] = full_ref[pl.ds(mine, heads), :]
        theirs_ref[...] = full_ref[pl.ds(heads - mine, heads), :]
    else:
        refs[0][...] = logits
    cum = decay_ref[...]
    lane = lax.broadcasted_iota(jnp.int32, cum.shape, 1)
    step = 1
    while step < cum.shape[1]:
        cum = cum + jnp.where(lane >= step, pltpu.roll(cum, step, 1), 0.0)
        step *= 2
    cum_ref[...] = cum
    keys = key_ref[...].astype(F32)
    squares = keys * keys
    rows = squares.shape[0]
    total_ref[...] = zeros_ref[...] + squares.reshape(rows // heads, heads, squares.shape[1]).sum(0)


def pack_kernel(
    groups, per, rank_ref, key_ref, value_ref, cum_ref, own_ref, came_ref, *refs
):
    out_refs, (beta_ref, flat_ref) = refs[:groups], refs[groups:]
    heads, n = cum_ref.shape
    beta_ref[...] = 1.0 / (1.0 + jnp.exp(-(own_ref[...] + came_ref[...])))
    for at, source in enumerate((key_ref, value_ref)):
        flat_ref[...] = source[...].astype(F32)
        for slot in range(groups):
            for i in range(per):
                head = (slot ^ rank_ref[0]) * per + i
                out_refs[slot][i, at * n : (at + 1) * n] = flat_ref[
                    pl.ds(head, n, stride=heads), :
                ]
    for slot in range(groups):
        for i in range(per):
            head = (slot ^ rank_ref[0]) * per + i
            out_refs[slot][i, 2 * n : 2 * n + 1] = cum_ref[pl.ds(head, 1), :]
            out_refs[slot][i, 2 * n + 1 : 2 * n + 2] = beta_ref[pl.ds(head, 1), :]
            out_refs[slot][i, 2 * n + 2 :] = jnp.zeros((6, n), F32)


def limits(total, tokens_all):
    return jnp.sqrt(jnp.sum(total, 1, keepdims=True) / tokens_all + EPSILON)


def solve(keys, values, cum, beta, limit, rows_ref):
    items, n = cum.shape
    row, col = iotas(n, n)
    keys_t = [key.T for key in keys]
    grams = [mm(key, key_t) for key, key_t in zip(keys, keys_t)]
    norm = jnp.concatenate(
        [jnp.sum(jnp.where(row == col, gram, 0.0), 0, keepdims=True) for gram in grams], 0
    )
    inverse = 1.0 / jnp.maximum(jnp.sqrt(norm), limit)
    for at, kind in enumerate((cum, beta * inverse, inverse)):
        rows_ref[at * items : (at + 1) * items, :] = kind
    columns = rows_ref[...].T

    def column(kind, item):
        at = kind * items + item
        return columns[:, at : at + 1]

    systems, inverses = [], []
    for item in range(items):
        spread = column(0, item) - cum[item : item + 1, :]
        damping = jnp.exp(jnp.where(row > col, spread, 0.0))
        system = jnp.where(
            row > col,
            grams[item] * damping * column(1, item) * inverse[item : item + 1, :],
            0.0,
        )
        systems.append(split(system))
        inverses.append(
            jnp.where(row == col, 1.0, jnp.where((row ^ col) == 1, -system, 0.0))
        )
    size = 2
    while size < n:
        joins = ((row ^ col) & ~(2 * size - 1)) == 0
        joins = joins & ((row & size) != 0) & ((col & size) == 0)
        parts = [split(x) for x in inverses]
        mids = [split(dot_square(a, x)) for a, x in zip(systems, parts)]
        ends = [dot_square(x, t) for x, t in zip(parts, mids)]
        inverses = [x - jnp.where(joins, e, 0.0) for x, e in zip(inverses, ends)]
        size *= 2
    write_scale = beta * jnp.exp(cum) * inverse
    writes = []
    for item in range(items):
        x, key, value = inverses[item], keys[item], values[item]
        w = mm(
            jnp.concatenate(split(x * write_scale[item : item + 1, :]), 1),
            jnp.concatenate([key, key], 0),
        )
        u = mm(
            jnp.concatenate(split(x * beta[item : item + 1, :]), 1),
            jnp.concatenate([value, value], 0),
        )
        writes.append(jnp.concatenate([w, u], 1) * column(2, item))
    return writes, keys_t, [column(0, item) for item in range(items)]


def read_map(write, key_t, carry, lift, row, col):
    d = key_t.shape[0]
    both = mm(
        jnp.concatenate([key_t, key_t], 1), jnp.concatenate(split(write * carry), 0)
    )
    ends = jnp.where(row == col, lift, 0.0)
    return jnp.concatenate([ends - both[:, :d], both[:, d:]], 1)


def chunk_maps(packs, per, tokens_all, rank_ref, total_ref, rows_ref):
    n = total_ref.shape[1]
    row, col = iotas(n, n)
    items = [(pack, i) for pack in packs for i in range(per)]
    limit = limits(total_ref[...], tokens_all)
    rows_ref[0 : limit.shape[0], :] = jnp.broadcast_to(limit, (limit.shape[0], n))
    limit = jnp.concatenate(
        [rows_ref[pl.ds(rank_ref[0] * per + i, 1), :] for _, i in items], 0
    )
    keys = [pack[i, 0:n].astype(BF16) for pack, i in items]
    values = [pack[i, n : 2 * n].astype(BF16) for pack, i in items]
    cum = jnp.concatenate([pack[i, 2 * n : 2 * n + 1] for pack, i in items], 0)
    beta = jnp.concatenate([pack[i, 2 * n + 1 : 2 * n + 2] for pack, i in items], 0)
    writes, keys_t, cum_columns = solve(keys, values, cum, beta, limit, rows_ref)
    maps = []
    for item in range(len(items)):
        last = cum[item : item + 1, n - 1 : n]
        maps.append(
            read_map(
                writes[item], keys_t[item], jnp.exp(last - cum_columns[item]), jnp.exp(last), row, col
            )
        )
    return maps


def run_kernel(groups, per, tokens_all, rank_ref, total_ref, *refs):
    packs, (prefix_ref, run_ref, rows_ref, held_ref) = refs[:groups], refs[groups:]
    for item, found in enumerate(chunk_maps(packs, per, tokens_all, rank_ref, total_ref, rows_ref)):
        held_ref[(item // per) ^ rank_ref[0], item % per] = found
    so_far = [held_ref[0, i] for i in range(per)]
    for place in range(1, groups):
        for i in range(per):
            prefix_ref[place - 1, i] = so_far[i]
        so_far = [join(held_ref[place, i], so_far[i]) for i in range(per)]
    for i in range(per):
        run_ref[i] = so_far[i]


def own_kernel(
    tokens_all, key_ref, value_ref, beta_ref, total_ref, cum_ref, wu_ref, flat_ref, rows_ref
):
    heads, n = cum_ref.shape
    flat_ref[...] = key_ref[...].astype(F32)
    keys = [flat_ref[pl.ds(h, n, stride=heads), :].astype(BF16) for h in range(heads)]
    flat_ref[...] = value_ref[...].astype(F32)
    values = [flat_ref[pl.ds(h, n, stride=heads), :].astype(BF16) for h in range(heads)]
    limit = limits(total_ref[...], tokens_all)
    writes, _, _ = solve(keys, values, cum_ref[...], beta_ref[...], limit, rows_ref)
    for h in range(heads):
        wu_ref[h] = writes[h]


def output_kernel(
    query_ref, key_ref, cum_ref, wu_ref, left_ref, right_ref, flat_ref, rows_ref
):
    heads, n = cum_ref.shape
    d = key_ref.shape[1]
    blocks = n // BLOCK
    row, col = iotas(n, n)
    cum = cum_ref[...]
    flat_ref[...] = key_ref[...].astype(F32)
    keys = [flat_ref[pl.ds(h, n, stride=heads), :].astype(BF16) for h in range(heads)]
    flat_ref[...] = query_ref[...].astype(F32)
    queries = [flat_ref[pl.ds(h, n, stride=heads), :] for h in range(heads)]
    position = lax.broadcasted_iota(jnp.int32, (heads, n), 1)
    kinds = [cum]
    for b in range(1, blocks):
        end = b * BLOCK
        fall = jnp.exp(jnp.minimum(cum[:, end - 1 : end] - cum, 0.0))
        kinds.append(jnp.where(position < end, fall, 0.0))
    for at, kind in enumerate(kinds):
        rows_ref[at * heads : (at + 1) * heads, :] = kind
    columns = rows_ref[...].T
    for h in range(heads):
        write, key_t, query = wu_ref[h], keys[h].T, queries[h]
        cum_column = columns[:, h : h + 1]
        reach = (
            1.0 / jnp.sqrt(jnp.sum(query * query, 1, keepdims=True) + EPSILON) * (d**-0.5)
        )
        scores = mm(query.astype(BF16), key_t)
        spread = jnp.where(row >= col, cum_column - cum[h : h + 1, :], 0.0)
        scores = jnp.where(row >= col, scores * jnp.exp(spread), 0.0) * reach
        both = dot_split(split(scores), split(write))
        rest = [query * (reach * jnp.exp(cum_column)) - both[:, :d]]
        outs = [both[:, d:]]
        for b in range(1, blocks):
            at = b * BLOCK - 1
            carry = columns[:, b * heads + h : b * heads + h + 1]
            inner = read_map(
                write, key_t, carry, jnp.exp(cum[h : h + 1, at : at + 1]), row, col
            )
            rest.append(inner[:, :d])
            outs.append(inner[:, d:])
        left_ref[h] = jnp.concatenate(split(jnp.concatenate(rest, 0)), 1)
        right_ref[h] = jnp.concatenate(outs, 0)


def join(latter, earlier):
    d = latter.shape[0]
    both = dot_split(split(latter[:, :d]), split(earlier))
    return jnp.concatenate([both[:, :d], both[:, d:] + latter[:, d:]], 1)


def apply(step, state):
    d = state.shape[0]
    return dot_split(split(step[:, :d]), split(state)) + step[:, d:]


def middle_kernel(per, upper_ref, mine_ref, other_ref, start_ref, state_ref):
    for i in range(per):
        mine, other = mine_ref[i], other_ref[i]
        upper = upper_ref[0] != 0
        earlier = jnp.where(upper, other, mine)
        latter = jnp.where(upper, mine, other)
        state_ref[i] = apply(latter, apply(earlier, start_ref[i]))


def reach_kernel(groups, per, upper_ref, prefix_ref, before_ref, step_ref, offset_ref):
    d = before_ref.shape[1]
    row, col = iotas(d, 2 * d)
    upper = upper_ref[0] != 0
    for i in range(per):
        before = before_ref[i]
        found = [jnp.where(upper, before, jnp.where(row == col, 1.0, 0.0))]
        for place in range(1, groups):
            prefix = prefix_ref[place - 1, i]
            found.append(jnp.where(upper, join(prefix, before), prefix))
        for place in range(groups):
            step_ref[place, i] = jnp.concatenate(split(found[place][:, :d]), 1)
            offset_ref[place, i] = found[place][:, d:]


def enter_kernel(groups, per, rank_ref, later_ref, step_ref, offset_ref, start_ref, came_ref, *refs):
    out_refs, (held_ref,) = refs[:groups], refs[groups:]
    d = start_ref.shape[1]
    for i in range(per):
        high, low = split(jnp.where(later_ref[0] != 0, came_ref[i], start_ref[i]))
        for place in range(groups):
            step = step_ref[place, i]
            held_ref[place ^ rank_ref[0], i] = (
                mm(step, jnp.concatenate([high, high], 0)) + mm(step[:, :d], low) + offset_ref[place, i]
            )
    for slot in range(groups):
        out_refs[slot][...] = held_ref[slot]


def finish_kernel(groups, per, rank_ref, *refs):
    states = refs[:groups]
    left_ref, right_ref, gate_ref, out_ref, block_ref, flat_ref, gates_ref = refs[groups:]
    heads = groups * per
    order = [(slot ^ rank_ref[0]) * per + i for slot in range(groups) for i in range(per)]
    d = gate_ref.shape[1]
    n = gate_ref.shape[0] // heads
    blocks = block_ref.shape[0]
    gates_ref[...] = gate_ref[...].astype(F32)
    for item, head in enumerate(order):
        state = states[item // per][item % per]
        high, low = split(state)
        left = left_ref[head]
        both = mm(left, jnp.concatenate([high, high], 0)) + mm(left[:, :d], low) + right_ref[head]
        raw = both[:n]
        block_ref[0, head] = state
        for b in range(1, blocks):
            block_ref[b, head] = both[n + (b - 1) * d : n + b * d]
        gate = gates_ref[pl.ds(head, n, stride=heads), :]
        scale = 1.0 / jnp.sqrt(jnp.mean(raw * raw, 1, keepdims=True) + EPSILON)
        flat_ref[pl.ds(head, n, stride=heads), :] = raw * scale * (gate / (1.0 + jnp.exp(-gate)))
    out_ref[...] = flat_ref[...].astype(BF16)


def exact(matrix, operand):
    return jnp.einsum("...ij,...jk->...ik", matrix, operand, precision=lax.Precision.HIGHEST)


def chain(latter, earlier):
    d = latter.shape[-2]
    both = exact(latter[..., :d], earlier)
    return jnp.concatenate([both[..., :d], both[..., d:] + latter[..., d:]], -1)


def flag(value):
    return jnp.reshape(value, (1,)).astype(jnp.int32)


def on_device(
    queries, key_vectors, values, out_gate, inputs, beta_weight, log_decay, initial_state
):
    n, heads, d = queries.shape
    blocks = n // BLOCK
    count, place = lax.axis_size("seq"), lax.axis_index("seq")
    groups = math.gcd(math.gcd(4, heads), count)
    per = heads // groups
    runs = count // groups
    rounds = runs.bit_length() - 1
    assert runs == 1 << rounds
    rank = flag(place % groups)
    run = place // groups

    def flipped(mask):
        return [(i, i ^ mask) for i in range(count)]

    def flat(tensor):
        return tensor.reshape(n * heads, d)

    pair = lax.axis_size("head") == 2
    all_heads = beta_weight.shape[0]
    zeros = call(zeros_kernel, shape(heads, d), flops=1 << 31)()
    total, cum, *logits = call(
        functools.partial(stats_kernel, heads, pair),
        [shape(heads, d), shape(heads, n)]
        + ([shape(heads, n)] * 2 if pair else [shape(all_heads, n)]),
        scratch=(pltpu.VMEM((all_heads, n), F32),) if pair else (),
        scalars=1,
        operands=5,
        flops=1 << 31,
    )(flag(lax.axis_index("head")), zeros, flat(key_vectors), beta_weight, inputs, log_decay)
    if pair:
        own, theirs = logits
        came = lax.ppermute(theirs, "head", [(0, 1), (1, 0)])
    else:
        own = lax.psum_scatter(logits[0], "head", scatter_dimension=0, tiled=True)
        came = jnp.zeros_like(own)
    packing = call(
        functools.partial(pack_kernel, groups, per),
        [shape(per, 2 * n + 8, d)] * groups + [shape(heads, n)],
        scratch=(pltpu.VMEM((n * heads, d), F32),),
        scalars=1,
        operands=5,
        flops=1 << 24,
    )
    *packs, beta = packing(rank, flat(key_vectors), flat(values), cum, own, came)

    def shared(total, mask):
        return lax.ppermute(total, "seq", flipped(mask))

    for slot in range(1, groups):
        if slot & (slot - 1) == 0:
            total = total + shared(total, slot)
    exchanged = []
    for slot in range(1, groups):
        exchanged.append(lax.ppermute(packs[slot], "seq", flipped(slot)))
    packs = [packs[0]] + exchanged
    mask = groups
    while mask < count:
        total = total + shared(total, mask)
        mask *= 2

    tokens_all = n * count
    prefix, run_map = call(
        functools.partial(run_kernel, groups, per, tokens_all),
        (shape(max(groups - 1, 1), per, d, 2 * d), shape(per, d, 2 * d)),
        scratch=(pltpu.VMEM((128, n), F32), pltpu.VMEM((groups, per, d, 2 * d), F32)),
        scalars=1,
        operands=1 + groups,
        flops=1 << 30,
    )(rank, total, *packs)

    wu = call(
        functools.partial(own_kernel, tokens_all),
        shape(heads, n, 2 * d),
        scratch=(pltpu.VMEM((n * heads, d), F32), pltpu.VMEM((128, n), F32)),
        operands=5,
        flops=1 << 31,
    )(flat(key_vectors), flat(values), beta, total, cum)

    start = lax.dynamic_slice_in_dim(initial_state, (place % groups) * per, per, 0)

    before, upper, came, later = run_map, flag(0), start, flag(0)
    if rounds == 2:
        other = lax.ppermute(run_map, "seq", flipped(groups))
        other, wu = lax.optimization_barrier((other, wu))
        upper = flag(run & 1)
        before = other
        middle = call(
            functools.partial(middle_kernel, per), shape(per, d, d), scalars=1, operands=3
        )(upper, run_map, other, start)
    elif rounds:
        eye = jnp.broadcast_to(jnp.eye(d, 2 * d, dtype=F32), run_map.shape)
        before, upper, window = eye, flag(1), run_map
        for r in range(rounds - 1):
            other = lax.ppermute(window, "seq", flipped(groups << r))
            high = (run >> r) & 1 == 1
            before = jnp.where(high, chain(before, other), before)
            window = chain(jnp.where(high, window, other), jnp.where(high, other, window))
        middle = exact(window[..., :d], start) + window[..., d:]
    if rounds:
        mirror = [(i, (runs - 1 - i // groups) * groups + i % groups) for i in range(count)]
        came = lax.ppermute(middle, "seq", mirror)
        later = flag(run >= runs // 2)
    rows = n + (blocks - 1) * d
    left, right = call(
        output_kernel,
        (shape(heads, rows, 2 * d, dtype=BF16), shape(heads, rows, d)),
        scratch=(pltpu.VMEM((n * heads, d), F32), pltpu.VMEM((128, n), F32)),
        operands=4,
        flops=1 << 30,
    )(flat(queries), flat(key_vectors), cum, wu)
    step, offset = call(
        functools.partial(reach_kernel, groups, per),
        (shape(groups, per, d, 2 * d, dtype=BF16), shape(groups, per, d, d)),
        scalars=1,
        operands=2,
        flops=1 << 28,
    )(upper, prefix, before)
    came, left, step = lax.optimization_barrier((came, left, step))
    entries = call(
        functools.partial(enter_kernel, groups, per),
        [shape(per, d, d)] * groups,
        scratch=(pltpu.VMEM((groups, per, d, d), F32),),
        scalars=2,
        operands=4,
        flops=1 << 27,
    )(rank, later, step, offset, start, came)

    states = [entries[0]] + [
        lax.ppermute(entries[slot], "seq", flipped(slot)) for slot in range(1, groups)
    ]
    gated, block_states = call(
        functools.partial(finish_kernel, groups, per),
        (shape(n * heads, d, dtype=BF16), shape(blocks, heads, d, d)),
        scratch=(pltpu.VMEM((n * heads, d), F32), pltpu.VMEM((n * heads, d), F32)),
        scalars=1,
        operands=groups + 3,
        flops=1 << 28,
    )(rank, *states, left, right, flat(out_gate))
    return (gated.reshape(n, heads, d), block_states)


def solution(mesh):
    return jax.shard_map(
        on_device,
        mesh=mesh,
        in_specs=(
            P("seq", "head", None),
            P("seq", "head", None),
            P("seq", "head", None),
            P("seq", "head", None),
            P("seq", "head"),
            P(None, "head"),
            P("head", "seq"),
            P("head", None, None),
        ),
        out_specs=(P("seq", "head", None), P("seq", "head", None, None)),
        check_vma=False,
    )
```

```python
import functools
import math

import jax
import jax.numpy as jnp
from jax import lax
from jax.experimental import pallas as pl
from jax.experimental.pallas import tpu as pltpu
from jax.sharding import PartitionSpec as P


BLOCK = 64
EPSILON = 1e-06
F32 = jnp.float32
BF16 = jnp.bfloat16
VMEM_LIMIT = 20 * 1024 * 1024


def split(x):
    high = x.astype(BF16)
    return high, (x - high.astype(F32)).astype(BF16)


def mm(a, b):
    return jnp.dot(a, b, preferred_element_type=F32)


def dot_split(left, right):
    (lh, ll), (rh, rl) = left, right
    return mm(jnp.concatenate([lh, ll], 1), jnp.concatenate([rh, rh], 0)) + mm(lh, rl)


def dot_square(left, right):
    (lh, ll), (rh, rl) = left, right
    n = rh.shape[1]
    wide = mm(
        jnp.concatenate([lh, ll], 1),
        jnp.concatenate(
            [jnp.concatenate([rh, rl], 1), jnp.concatenate([rh, jnp.zeros_like(rl)], 1)], 0
        ),
    )
    return wide[:, :n] + wide[:, n:]


def iotas(n, m):
    return (
        lax.broadcasted_iota(jnp.int32, (n, m), 0),
        lax.broadcasted_iota(jnp.int32, (n, m), 1),
    )


def vmem(count):
    return [pl.BlockSpec(memory_space=pltpu.VMEM)] * count


def smem():
    return pl.BlockSpec(memory_space=pltpu.SMEM)


def call(kernel, out_shape, scratch=(), scalars=0, operands=0, anywhere=0, flops=0, grant=VMEM_LIMIT):
    single = not isinstance(out_shape, (list, tuple))
    return pl.pallas_call(
        kernel,
        out_shape=out_shape,
        in_specs=[smem()] * scalars
        + [pl.BlockSpec(memory_space=pltpu.HBM)] * anywhere
        + vmem(operands),
        out_specs=vmem(1)[0] if single else vmem(len(out_shape)),
        scratch_shapes=list(scratch),
        compiler_params=pltpu.CompilerParams(vmem_limit_bytes=grant),
        cost_estimate=pl.CostEstimate(flops=flops, bytes_accessed=1 << 20, transcendentals=0),
    )


def shape(*dims, dtype=F32):
    return jax.ShapeDtypeStruct(dims, dtype)


def zeros_kernel(out_ref):
    out_ref[...] = jnp.zeros_like(out_ref)


def stats_kernel(
    heads, pair, side_ref, zeros_ref, key_ref, weight_ref, inputs_ref, decay_ref, total_ref, cum_ref, *refs
):
    logits = lax.dot_general(
        weight_ref[...], inputs_ref[...], (((1,), (1,)), ((), ())), preferred_element_type=F32
    )
    if pair:
        own_ref, theirs_ref, full_ref = refs
        full_ref[...] = logits
        mine = pl.multiple_of(side_ref[0] * heads, heads)
        own_ref[...] = full_ref[pl.ds(mine, heads), :]
        theirs_ref[...] = full_ref[pl.ds(heads - mine, heads), :]
    else:
        refs[0][...] = logits
    cum = decay_ref[...]
    lane = lax.broadcasted_iota(jnp.int32, cum.shape, 1)
    step = 1
    while step < cum.shape[1]:
        cum = cum + jnp.where(lane >= step, pltpu.roll(cum, step, 1), 0.0)
        step *= 2
    cum_ref[...] = cum
    keys = key_ref[...].astype(F32)
    squares = keys * keys
    rows = squares.shape[0]
    total_ref[...] = zeros_ref[...] + squares.reshape(rows // heads, heads, squares.shape[1]).sum(0)


def pack_kernel(
    groups, per, rank_ref, key_ref, value_ref, cum_ref, own_ref, came_ref, *refs
):
    out_refs, (beta_ref, flat_ref) = refs[:groups], refs[groups:]
    heads, n = cum_ref.shape
    beta_ref[...] = 1.0 / (1.0 + jnp.exp(-(own_ref[...] + came_ref[...])))
    for at, source in enumerate((key_ref, value_ref)):
        flat_ref[...] = source[...].astype(F32)
        for slot in range(groups):
            for i in range(per):
                head = (slot ^ rank_ref[0]) * per + i
                out_refs[slot][i, at * n : (at + 1) * n] = flat_ref[
                    pl.ds(head, n, stride=heads), :
                ]
    for slot in range(groups):
        for i in range(per):
            head = (slot ^ rank_ref[0]) * per + i
            out_refs[slot][i, 2 * n : 2 * n + 1] = cum_ref[pl.ds(head, 1), :]
            out_refs[slot][i, 2 * n + 1 : 2 * n + 2] = beta_ref[pl.ds(head, 1), :]
            out_refs[slot][i, 2 * n + 2 :] = jnp.zeros((6, n), F32)


def limits(total, tokens_all):
    return jnp.sqrt(jnp.sum(total, 1, keepdims=True) / tokens_all + EPSILON)


def solve(keys, values, cum, beta, limit, rows_ref):
    items, n = cum.shape
    row, col = iotas(n, n)
    keys_t = [key.T for key in keys]
    grams = [mm(key, key_t) for key, key_t in zip(keys, keys_t)]
    norm = jnp.concatenate(
        [jnp.sum(jnp.where(row == col, gram, 0.0), 0, keepdims=True) for gram in grams], 0
    )
    inverse = 1.0 / jnp.maximum(jnp.sqrt(norm), limit)
    for at, kind in enumerate((cum, beta * inverse, inverse)):
        rows_ref[at * items : (at + 1) * items, :] = kind
    columns = rows_ref[...].T

    def column(kind, item):
        at = kind * items + item
        return columns[:, at : at + 1]

    systems, inverses = [], []
    for item in range(items):
        spread = column(0, item) - cum[item : item + 1, :]
        damping = jnp.exp(jnp.where(row > col, spread, 0.0))
        system = jnp.where(
            row > col,
            grams[item] * damping * column(1, item) * inverse[item : item + 1, :],
            0.0,
        )
        systems.append(split(system))
        inverses.append(
            jnp.where(row == col, 1.0, jnp.where((row ^ col) == 1, -system, 0.0))
        )
    size = 2
    while size < n:
        grown = 4 * size if 4 * size <= n else 2 * size
        joins = (((row ^ col) & ~(grown - 1)) == 0) & (((row ^ col) & ~(size - 1)) != 0)
        parts = [split(x) for x in inverses]
        mixes = [jnp.where(joins, dot_square(x, a), 0.0) for x, a in zip(parts, systems)]
        mixes = [split(mix) for mix in mixes]
        inverses = [x - dot_square(mix, part) for x, mix, part in zip(inverses, mixes, parts)]
        if grown == 4 * size:
            squares = [split(dot_square(mix, mix)) for mix in mixes]
            inverses = [x + dot_square(sq, split(x)) for x, sq in zip(inverses, squares)]
        size = grown
    write_scale = beta * jnp.exp(cum) * inverse
    writes = []
    for item in range(items):
        x, key, value = inverses[item], keys[item], values[item]
        w = mm(
            jnp.concatenate(split(x * write_scale[item : item + 1, :]), 1),
            jnp.concatenate([key, key], 0),
        )
        u = mm(
            jnp.concatenate(split(x * beta[item : item + 1, :]), 1),
            jnp.concatenate([value, value], 0),
        )
        writes.append(jnp.concatenate([w, u], 1) * column(2, item))
    return writes, keys_t, [column(0, item) for item in range(items)]


def read_map(write, key_t, carry, lift, row, col):
    d = key_t.shape[0]
    both = mm(
        jnp.concatenate([key_t, key_t], 1), jnp.concatenate(split(write * carry), 0)
    )
    ends = jnp.where(row == col, lift, 0.0)
    return jnp.concatenate([ends - both[:, :d], both[:, d:]], 1)


def chunk_maps(packs, per, tokens_all, rank_ref, total_ref, rows_ref):
    n = total_ref.shape[1]
    row, col = iotas(n, n)
    items = [(pack, i) for pack in packs for i in range(per)]
    limit = limits(total_ref[...], tokens_all)
    rows_ref[0 : limit.shape[0], :] = jnp.broadcast_to(limit, (limit.shape[0], n))
    limit = jnp.concatenate(
        [rows_ref[pl.ds(rank_ref[0] * per + i, 1), :] for _, i in items], 0
    )
    keys = [pack[i, 0:n].astype(BF16) for pack, i in items]
    values = [pack[i, n : 2 * n].astype(BF16) for pack, i in items]
    cum = jnp.concatenate([pack[i, 2 * n : 2 * n + 1] for pack, i in items], 0)
    beta = jnp.concatenate([pack[i, 2 * n + 1 : 2 * n + 2] for pack, i in items], 0)
    writes, keys_t, cum_columns = solve(keys, values, cum, beta, limit, rows_ref)
    maps = []
    for item in range(len(items)):
        last = cum[item : item + 1, n - 1 : n]
        maps.append(
            read_map(
                writes[item], keys_t[item], jnp.exp(last - cum_columns[item]), jnp.exp(last), row, col
            )
        )
    return maps


def run_kernel(groups, per, tokens_all, rank_ref, total_ref, *refs):
    packs, (prefix_ref, run_ref, rows_ref, held_ref) = refs[:groups], refs[groups:]
    for item, found in enumerate(chunk_maps(packs, per, tokens_all, rank_ref, total_ref, rows_ref)):
        held_ref[(item // per) ^ rank_ref[0], item % per] = found
    so_far = [held_ref[0, i] for i in range(per)]
    for place in range(1, groups):
        for i in range(per):
            prefix_ref[place - 1, i] = so_far[i]
        so_far = [join(held_ref[place, i], so_far[i]) for i in range(per)]
    for i in range(per):
        run_ref[i] = so_far[i]


def own_kernel(
    tokens_all, key_ref, value_ref, beta_ref, total_ref, cum_ref, wu_ref, flat_ref, rows_ref
):
    heads, n = cum_ref.shape
    flat_ref[...] = key_ref[...].astype(F32)
    keys = [flat_ref[pl.ds(h, n, stride=heads), :].astype(BF16) for h in range(heads)]
    flat_ref[...] = value_ref[...].astype(F32)
    values = [flat_ref[pl.ds(h, n, stride=heads), :].astype(BF16) for h in range(heads)]
    limit = limits(total_ref[...], tokens_all)
    writes, _, _ = solve(keys, values, cum_ref[...], beta_ref[...], limit, rows_ref)
    for h in range(heads):
        wu_ref[h] = writes[h]


def output_kernel(
    query_ref, key_ref, cum_ref, wu_ref, left_ref, right_ref, flat_ref, rows_ref
):
    heads, n = cum_ref.shape
    d = key_ref.shape[1]
    blocks = n // BLOCK
    row, col = iotas(n, n)
    cum = cum_ref[...]
    flat_ref[...] = key_ref[...].astype(F32)
    keys = [flat_ref[pl.ds(h, n, stride=heads), :].astype(BF16) for h in range(heads)]
    flat_ref[...] = query_ref[...].astype(F32)
    queries = [flat_ref[pl.ds(h, n, stride=heads), :] for h in range(heads)]
    position = lax.broadcasted_iota(jnp.int32, (heads, n), 1)
    kinds = [cum]
    for b in range(1, blocks):
        end = b * BLOCK
        fall = jnp.exp(jnp.minimum(cum[:, end - 1 : end] - cum, 0.0))
        kinds.append(jnp.where(position < end, fall, 0.0))
    for at, kind in enumerate(kinds):
        rows_ref[at * heads : (at + 1) * heads, :] = kind
    columns = rows_ref[...].T
    for h in range(heads):
        write, key_t, query = wu_ref[h], keys[h].T, queries[h]
        cum_column = columns[:, h : h + 1]
        reach = (
            1.0 / jnp.sqrt(jnp.sum(query * query, 1, keepdims=True) + EPSILON) * (d**-0.5)
        )
        scores = mm(query.astype(BF16), key_t)
        spread = jnp.where(row >= col, cum_column - cum[h : h + 1, :], 0.0)
        scores = jnp.where(row >= col, scores * jnp.exp(spread), 0.0) * reach
        both = dot_split(split(scores), split(write))
        rest = [query * (reach * jnp.exp(cum_column)) - both[:, :d]]
        outs = [both[:, d:]]
        for b in range(1, blocks):
            at = b * BLOCK - 1
            carry = columns[:, b * heads + h : b * heads + h + 1]
            inner = read_map(
                write, key_t, carry, jnp.exp(cum[h : h + 1, at : at + 1]), row, col
            )
            rest.append(inner[:, :d])
            outs.append(inner[:, d:])
        left_ref[h] = jnp.concatenate(split(jnp.concatenate(rest, 0)), 1)
        right_ref[h] = jnp.concatenate(outs, 0)


def join(latter, earlier):
    d = latter.shape[0]
    both = dot_split(split(latter[:, :d]), split(earlier))
    return jnp.concatenate([both[:, :d], both[:, d:] + latter[:, d:]], 1)


def apply(step, state):
    d = state.shape[0]
    return dot_split(split(step[:, :d]), split(state)) + step[:, d:]


def middle_kernel(per, upper_ref, mine_ref, other_ref, start_ref, state_ref):
    for i in range(per):
        mine, other = mine_ref[i], other_ref[i]
        upper = upper_ref[0] != 0
        earlier = jnp.where(upper, other, mine)
        latter = jnp.where(upper, mine, other)
        state_ref[i] = apply(latter, apply(earlier, start_ref[i]))


def reach_kernel(groups, per, upper_ref, prefix_ref, before_ref, step_ref, offset_ref):
    d = before_ref.shape[1]
    row, col = iotas(d, 2 * d)
    upper = upper_ref[0] != 0
    for i in range(per):
        before = before_ref[i]
        found = [jnp.where(upper, before, jnp.where(row == col, 1.0, 0.0))]
        for place in range(1, groups):
            prefix = prefix_ref[place - 1, i]
            found.append(jnp.where(upper, join(prefix, before), prefix))
        for place in range(groups):
            step_ref[place, i] = jnp.concatenate(split(found[place][:, :d]), 1)
            offset_ref[place, i] = found[place][:, d:]


def enter_kernel(groups, per, rank_ref, later_ref, step_ref, offset_ref, start_ref, came_ref, *refs):
    out_refs, (held_ref,) = refs[:groups], refs[groups:]
    d = start_ref.shape[1]
    for i in range(per):
        high, low = split(jnp.where(later_ref[0] != 0, came_ref[i], start_ref[i]))
        for place in range(groups):
            step = step_ref[place, i]
            held_ref[place ^ rank_ref[0], i] = (
                mm(step, jnp.concatenate([high, high], 0)) + mm(step[:, :d], low) + offset_ref[place, i]
            )
    for slot in range(groups):
        out_refs[slot][...] = held_ref[slot]


def finish_kernel(groups, per, rank_ref, *refs):
    states = refs[:groups]
    left_ref, right_ref, gate_ref, out_ref, block_ref, flat_ref, gates_ref = refs[groups:]
    heads = groups * per
    order = [(slot ^ rank_ref[0]) * per + i for slot in range(groups) for i in range(per)]
    d = gate_ref.shape[1]
    n = gate_ref.shape[0] // heads
    blocks = block_ref.shape[0]
    gates_ref[...] = gate_ref[...].astype(F32)
    for item, head in enumerate(order):
        state = states[item // per][item % per]
        high, low = split(state)
        left = left_ref[head]
        both = mm(left, jnp.concatenate([high, high], 0)) + mm(left[:, :d], low) + right_ref[head]
        raw = both[:n]
        block_ref[0, head] = state
        for b in range(1, blocks):
            block_ref[b, head] = both[n + (b - 1) * d : n + b * d]
        gate = gates_ref[pl.ds(head, n, stride=heads), :]
        scale = 1.0 / jnp.sqrt(jnp.mean(raw * raw, 1, keepdims=True) + EPSILON)
        flat_ref[pl.ds(head, n, stride=heads), :] = raw * scale * (gate / (1.0 + jnp.exp(-gate)))
    out_ref[...] = flat_ref[...].astype(BF16)


def exact(matrix, operand):
    return jnp.einsum("...ij,...jk->...ik", matrix, operand, precision=lax.Precision.HIGHEST)


def chain(latter, earlier):
    d = latter.shape[-2]
    both = exact(latter[..., :d], earlier)
    return jnp.concatenate([both[..., :d], both[..., d:] + latter[..., d:]], -1)


def flag(value):
    return jnp.reshape(value, (1,)).astype(jnp.int32)


def on_device(
    queries, key_vectors, values, out_gate, inputs, beta_weight, log_decay, initial_state
):
    n, heads, d = queries.shape
    blocks = n // BLOCK
    count, place = lax.axis_size("seq"), lax.axis_index("seq")
    groups = math.gcd(math.gcd(4, heads), count)
    per = heads // groups
    runs = count // groups
    rounds = runs.bit_length() - 1
    assert runs == 1 << rounds
    rank = flag(place % groups)
    run = place // groups

    def flipped(mask):
        return [(i, i ^ mask) for i in range(count)]

    def flat(tensor):
        return tensor.reshape(n * heads, d)

    pair = lax.axis_size("head") == 2
    all_heads = beta_weight.shape[0]
    zeros = call(zeros_kernel, shape(heads, d), flops=1 << 31)()
    total, cum, *logits = call(
        functools.partial(stats_kernel, heads, pair),
        [shape(heads, d), shape(heads, n)]
        + ([shape(heads, n)] * 2 if pair else [shape(all_heads, n)]),
        scratch=(pltpu.VMEM((all_heads, n), F32),) if pair else (),
        scalars=1,
        operands=5,
        flops=1 << 31,
    )(flag(lax.axis_index("head")), zeros, flat(key_vectors), beta_weight, inputs, log_decay)
    if pair:
        own, theirs = logits
        came = lax.ppermute(theirs, "head", [(0, 1), (1, 0)])
    else:
        own = lax.psum_scatter(logits[0], "head", scatter_dimension=0, tiled=True)
        came = jnp.zeros_like(own)
    packing = call(
        functools.partial(pack_kernel, groups, per),
        [shape(per, 2 * n + 8, d)] * groups + [shape(heads, n)],
        scratch=(pltpu.VMEM((n * heads, d), F32),),
        scalars=1,
        operands=5,
        flops=1 << 24,
    )
    *packs, beta = packing(rank, flat(key_vectors), flat(values), cum, own, came)

    def shared(total, mask):
        return lax.ppermute(total, "seq", flipped(mask))

    for slot in range(1, groups):
        if slot & (slot - 1) == 0:
            total = total + shared(total, slot)
    exchanged = []
    for slot in range(1, groups):
        exchanged.append(lax.ppermute(packs[slot], "seq", flipped(slot)))
    packs = [packs[0]] + exchanged
    mask = groups
    while mask < count:
        total = total + shared(total, mask)
        mask *= 2

    tokens_all = n * count
    prefix, run_map = call(
        functools.partial(run_kernel, groups, per, tokens_all),
        (shape(max(groups - 1, 1), per, d, 2 * d), shape(per, d, 2 * d)),
        scratch=(pltpu.VMEM((128, n), F32), pltpu.VMEM((groups, per, d, 2 * d), F32)),
        scalars=1,
        operands=1 + groups,
        flops=1 << 30,
    )(rank, total, *packs)

    wu = call(
        functools.partial(own_kernel, tokens_all),
        shape(heads, n, 2 * d),
        scratch=(pltpu.VMEM((n * heads, d), F32), pltpu.VMEM((128, n), F32)),
        operands=5,
        flops=1 << 31,
    )(flat(key_vectors), flat(values), beta, total, cum)

    start = lax.dynamic_slice_in_dim(initial_state, (place % groups) * per, per, 0)

    before, upper, came, later = run_map, flag(0), start, flag(0)
    if rounds == 2:
        other = lax.ppermute(run_map, "seq", flipped(groups))
        other, wu = lax.optimization_barrier((other, wu))
        upper = flag(run & 1)
        before = other
        middle = call(
            functools.partial(middle_kernel, per), shape(per, d, d), scalars=1, operands=3
        )(upper, run_map, other, start)
    elif rounds:
        eye = jnp.broadcast_to(jnp.eye(d, 2 * d, dtype=F32), run_map.shape)
        before, upper, window = eye, flag(1), run_map
        for r in range(rounds - 1):
            other = lax.ppermute(window, "seq", flipped(groups << r))
            high = (run >> r) & 1 == 1
            before = jnp.where(high, chain(before, other), before)
            window = chain(jnp.where(high, window, other), jnp.where(high, other, window))
        middle = exact(window[..., :d], start) + window[..., d:]
    if rounds:
        mirror = [(i, (runs - 1 - i // groups) * groups + i % groups) for i in range(count)]
        came = lax.ppermute(middle, "seq", mirror)
        later = flag(run >= runs // 2)
    rows = n + (blocks - 1) * d
    left, right = call(
        output_kernel,
        (shape(heads, rows, 2 * d, dtype=BF16), shape(heads, rows, d)),
        scratch=(pltpu.VMEM((n * heads, d), F32), pltpu.VMEM((128, n), F32)),
        operands=4,
        flops=1 << 30,
    )(flat(queries), flat(key_vectors), cum, wu)
    step, offset = call(
        functools.partial(reach_kernel, groups, per),
        (shape(groups, per, d, 2 * d, dtype=BF16), shape(groups, per, d, d)),
        scalars=1,
        operands=2,
        flops=1 << 28,
    )(upper, prefix, before)
    came, left, step = lax.optimization_barrier((came, left, step))
    entries = call(
        functools.partial(enter_kernel, groups, per),
        [shape(per, d, d)] * groups,
        scratch=(pltpu.VMEM((groups, per, d, d), F32),),
        scalars=2,
        operands=4,
        flops=1 << 27,
    )(rank, later, step, offset, start, came)

    states = [entries[0]] + [
        lax.ppermute(entries[slot], "seq", flipped(slot)) for slot in range(1, groups)
    ]
    gated, block_states = call(
        functools.partial(finish_kernel, groups, per),
        (shape(n * heads, d, dtype=BF16), shape(blocks, heads, d, d)),
        scratch=(pltpu.VMEM((n * heads, d), F32), pltpu.VMEM((n * heads, d), F32)),
        scalars=1,
        operands=groups + 3,
        flops=1 << 28,
    )(rank, *states, left, right, flat(out_gate))
    return (gated.reshape(n, heads, d), block_states)


def solution(mesh):
    return jax.shard_map(
        on_device,
        mesh=mesh,
        in_specs=(
            P("seq", "head", None),
            P("seq", "head", None),
            P("seq", "head", None),
            P("seq", "head", None),
            P("seq", "head"),
            P(None, "head"),
            P("head", "seq"),
            P("head", None, None),
        ),
        out_specs=(P("seq", "head", None), P("seq", "head", None, None)),
        check_vma=False,
    )
```

```python
import functools
import math

import jax
import jax.numpy as jnp
from jax import lax
from jax.experimental import pallas as pl
from jax.experimental.pallas import tpu as pltpu
from jax.sharding import PartitionSpec as P


BLOCK = 64
EPSILON = 1e-06
F32 = jnp.float32
BF16 = jnp.bfloat16
VMEM_LIMIT = 20 * 1024 * 1024
PIECES = 4
EARLY = (0, 3)


def split(x):
    high = x.astype(BF16)
    return high, (x - high.astype(F32)).astype(BF16)


def mm(a, b):
    return jnp.dot(a, b, preferred_element_type=F32)


def dot_split(left, right):
    (lh, ll), (rh, rl) = left, right
    return mm(jnp.concatenate([lh, ll], 1), jnp.concatenate([rh, rh], 0)) + mm(lh, rl)


def dot_square(left, right):
    (lh, ll), (rh, rl) = left, right
    n = rh.shape[1]
    wide = mm(
        jnp.concatenate([lh, ll], 1),
        jnp.concatenate(
            [jnp.concatenate([rh, rl], 1), jnp.concatenate([rh, jnp.zeros_like(rl)], 1)], 0
        ),
    )
    return wide[:, :n] + wide[:, n:]


def iotas(n, m):
    return (
        lax.broadcasted_iota(jnp.int32, (n, m), 0),
        lax.broadcasted_iota(jnp.int32, (n, m), 1),
    )


def vmem(count):
    return [pl.BlockSpec(memory_space=pltpu.VMEM)] * count


def smem():
    return pl.BlockSpec(memory_space=pltpu.SMEM)


def call(kernel, out_shape, scratch=(), scalars=0, operands=0, anywhere=0, flops=0, grant=VMEM_LIMIT):
    single = not isinstance(out_shape, (list, tuple))
    return pl.pallas_call(
        kernel,
        out_shape=out_shape,
        in_specs=[smem()] * scalars
        + [pl.BlockSpec(memory_space=pltpu.HBM)] * anywhere
        + vmem(operands),
        out_specs=vmem(1)[0] if single else vmem(len(out_shape)),
        scratch_shapes=list(scratch),
        compiler_params=pltpu.CompilerParams(vmem_limit_bytes=grant),
        cost_estimate=pl.CostEstimate(flops=flops, bytes_accessed=1 << 20, transcendentals=0),
    )


def shape(*dims, dtype=F32):
    return jax.ShapeDtypeStruct(dims, dtype)


def zeros_kernel(out_ref):
    out_ref[...] = jnp.zeros_like(out_ref)


def stats_kernel(
    heads, pair, side_ref, zeros_ref, key_ref, weight_ref, inputs_ref, decay_ref, total_ref, cum_ref, *refs
):
    logits = lax.dot_general(
        weight_ref[...], inputs_ref[...], (((1,), (1,)), ((), ())), preferred_element_type=F32
    )
    if pair:
        own_ref, theirs_ref, full_ref = refs
        full_ref[...] = logits
        mine = pl.multiple_of(side_ref[0] * heads, heads)
        own_ref[...] = full_ref[pl.ds(mine, heads), :]
        theirs_ref[...] = full_ref[pl.ds(heads - mine, heads), :]
    else:
        refs[0][...] = logits
    cum = decay_ref[...]
    lane = lax.broadcasted_iota(jnp.int32, cum.shape, 1)
    step = 1
    while step < cum.shape[1]:
        cum = cum + jnp.where(lane >= step, pltpu.roll(cum, step, 1), 0.0)
        step *= 2
    cum_ref[...] = cum
    keys = key_ref[...].astype(F32)
    squares = keys * keys
    rows = squares.shape[0]
    total_ref[...] = zeros_ref[...] + squares.reshape(rows // heads, heads, squares.shape[1]).sum(0)


def pack_kernel(
    groups, per, rank_ref, key_ref, value_ref, cum_ref, own_ref, came_ref, *refs
):
    out_refs, (beta_ref, flat_ref) = refs[:groups], refs[groups:]
    heads, n = cum_ref.shape
    beta_ref[...] = 1.0 / (1.0 + jnp.exp(-(own_ref[...] + came_ref[...])))
    for at, source in enumerate((key_ref, value_ref)):
        flat_ref[...] = source[...].astype(F32)
        for slot in range(groups):
            for i in range(per):
                head = (slot ^ rank_ref[0]) * per + i
                out_refs[slot][i, at * n : (at + 1) * n] = flat_ref[
                    pl.ds(head, n, stride=heads), :
                ]
    for slot in range(groups):
        for i in range(per):
            head = (slot ^ rank_ref[0]) * per + i
            out_refs[slot][i, 2 * n : 2 * n + 1] = cum_ref[pl.ds(head, 1), :]
            out_refs[slot][i, 2 * n + 1 : 2 * n + 2] = beta_ref[pl.ds(head, 1), :]
            out_refs[slot][i, 2 * n + 2 :] = jnp.zeros((6, n), F32)


def limits(total, tokens_all):
    return jnp.sqrt(jnp.sum(total, 1, keepdims=True) / tokens_all + EPSILON)


def solve(keys, values, cum, beta, limit, rows_ref):
    items, n = cum.shape
    row, col = iotas(n, n)
    keys_t = [key.T for key in keys]
    grams = [mm(key, key_t) for key, key_t in zip(keys, keys_t)]
    norm = jnp.concatenate(
        [jnp.sum(jnp.where(row == col, gram, 0.0), 0, keepdims=True) for gram in grams], 0
    )
    inverse = 1.0 / jnp.maximum(jnp.sqrt(norm), limit)
    for at, kind in enumerate((cum, beta * inverse, inverse)):
        rows_ref[at * items : (at + 1) * items, :] = kind
    columns = rows_ref[...].T

    def column(kind, item):
        at = kind * items + item
        return columns[:, at : at + 1]

    systems, inverses = [], []
    for item in range(items):
        spread = column(0, item) - cum[item : item + 1, :]
        damping = jnp.exp(jnp.where(row > col, spread, 0.0))
        system = jnp.where(
            row > col,
            grams[item] * damping * column(1, item) * inverse[item : item + 1, :],
            0.0,
        )
        systems.append(split(system))
        inverses.append(
            jnp.where(row == col, 1.0, jnp.where((row ^ col) == 1, -system, 0.0))
        )
    size = 2
    while size < n:
        grown = 4 * size if 4 * size <= n else 2 * size
        joins = (((row ^ col) & ~(grown - 1)) == 0) & (((row ^ col) & ~(size - 1)) != 0)
        parts = [split(x) for x in inverses]
        mixes = [jnp.where(joins, dot_square(x, a), 0.0) for x, a in zip(parts, systems)]
        mixes = [split(mix) for mix in mixes]
        inverses = [x - dot_square(mix, part) for x, mix, part in zip(inverses, mixes, parts)]
        if grown == 4 * size:
            squares = [split(dot_square(mix, mix)) for mix in mixes]
            inverses = [x + dot_square(sq, split(x)) for x, sq in zip(inverses, squares)]
        size = grown
    write_scale = beta * jnp.exp(cum) * inverse
    writes = []
    for item in range(items):
        x, key, value = inverses[item], keys[item], values[item]
        w = mm(
            jnp.concatenate(split(x * write_scale[item : item + 1, :]), 1),
            jnp.concatenate([key, key], 0),
        )
        u = mm(
            jnp.concatenate(split(x * beta[item : item + 1, :]), 1),
            jnp.concatenate([value, value], 0),
        )
        writes.append(jnp.concatenate([w, u], 1) * column(2, item))
    return writes, keys_t, [column(0, item) for item in range(items)]


def read_map(write, key_t, carry, lift, row, col):
    d = key_t.shape[0]
    both = mm(
        jnp.concatenate([key_t, key_t], 1), jnp.concatenate(split(write * carry), 0)
    )
    ends = jnp.where(row == col, lift, 0.0)
    return jnp.concatenate([ends - both[:, :d], both[:, d:]], 1)


def chunk_maps(packs, per, tokens_all, rank_ref, total_ref, rows_ref):
    n = total_ref.shape[1]
    row, col = iotas(n, n)
    items = [(pack, i) for pack in packs for i in range(per)]
    limit = limits(total_ref[...], tokens_all)
    rows_ref[0 : limit.shape[0], :] = jnp.broadcast_to(limit, (limit.shape[0], n))
    limit = jnp.concatenate(
        [rows_ref[pl.ds(rank_ref[0] * per + i, 1), :] for _, i in items], 0
    )
    keys = [pack[i, 0:n].astype(BF16) for pack, i in items]
    values = [pack[i, n : 2 * n].astype(BF16) for pack, i in items]
    cum = jnp.concatenate([pack[i, 2 * n : 2 * n + 1] for pack, i in items], 0)
    beta = jnp.concatenate([pack[i, 2 * n + 1 : 2 * n + 2] for pack, i in items], 0)
    writes, keys_t, cum_columns = solve(keys, values, cum, beta, limit, rows_ref)
    maps = []
    for item in range(len(items)):
        last = cum[item : item + 1, n - 1 : n]
        maps.append(
            read_map(
                writes[item], keys_t[item], jnp.exp(last - cum_columns[item]), jnp.exp(last), row, col
            )
        )
    return maps


def run_kernel(groups, per, tokens_all, rank_ref, total_ref, *refs):
    packs, (prefix_ref, run_ref, rows_ref, held_ref) = refs[:groups], refs[groups:]
    for item, found in enumerate(chunk_maps(packs, per, tokens_all, rank_ref, total_ref, rows_ref)):
        held_ref[(item // per) ^ rank_ref[0], item % per] = found
    so_far = [held_ref[0, i] for i in range(per)]
    for place in range(1, groups):
        for i in range(per):
            prefix_ref[place - 1, i] = so_far[i]
        so_far = [join(held_ref[place, i], so_far[i]) for i in range(per)]
    for i in range(per):
        run_ref[i] = so_far[i]


def own_kernel(
    tokens_all, key_ref, value_ref, beta_ref, total_ref, cum_ref, wu_ref, flat_ref, rows_ref
):
    heads, n = cum_ref.shape
    flat_ref[...] = key_ref[...].astype(F32)
    keys = [flat_ref[pl.ds(h, n, stride=heads), :].astype(BF16) for h in range(heads)]
    flat_ref[...] = value_ref[...].astype(F32)
    values = [flat_ref[pl.ds(h, n, stride=heads), :].astype(BF16) for h in range(heads)]
    limit = limits(total_ref[...], tokens_all)
    writes, _, _ = solve(keys, values, cum_ref[...], beta_ref[...], limit, rows_ref)
    for h in range(heads):
        wu_ref[h] = writes[h]


def output_kernel(
    query_ref, key_ref, cum_ref, wu_ref, left_ref, right_ref, flat_ref, rows_ref
):
    heads, n = cum_ref.shape
    d = key_ref.shape[1]
    blocks = n // BLOCK
    row, col = iotas(n, n)
    cum = cum_ref[...]
    flat_ref[...] = key_ref[...].astype(F32)
    keys = [flat_ref[pl.ds(h, n, stride=heads), :].astype(BF16) for h in range(heads)]
    flat_ref[...] = query_ref[...].astype(F32)
    queries = [flat_ref[pl.ds(h, n, stride=heads), :] for h in range(heads)]
    position = lax.broadcasted_iota(jnp.int32, (heads, n), 1)
    kinds = [cum]
    for b in range(1, blocks):
        end = b * BLOCK
        fall = jnp.exp(jnp.minimum(cum[:, end - 1 : end] - cum, 0.0))
        kinds.append(jnp.where(position < end, fall, 0.0))
    for at, kind in enumerate(kinds):
        rows_ref[at * heads : (at + 1) * heads, :] = kind
    columns = rows_ref[...].T
    for h in range(heads):
        write, key_t, query = wu_ref[h], keys[h].T, queries[h]
        cum_column = columns[:, h : h + 1]
        reach = (
            1.0 / jnp.sqrt(jnp.sum(query * query, 1, keepdims=True) + EPSILON) * (d**-0.5)
        )
        scores = mm(query.astype(BF16), key_t)
        spread = jnp.where(row >= col, cum_column - cum[h : h + 1, :], 0.0)
        scores = jnp.where(row >= col, scores * jnp.exp(spread), 0.0) * reach
        both = dot_split(split(scores), split(write))
        rest = [query * (reach * jnp.exp(cum_column)) - both[:, :d]]
        outs = [both[:, d:]]
        for b in range(1, blocks):
            at = b * BLOCK - 1
            carry = columns[:, b * heads + h : b * heads + h + 1]
            inner = read_map(
                write, key_t, carry, jnp.exp(cum[h : h + 1, at : at + 1]), row, col
            )
            rest.append(inner[:, :d])
            outs.append(inner[:, d:])
        left_ref[h] = jnp.concatenate(split(jnp.concatenate(rest, 0)), 1)
        right_ref[h] = jnp.concatenate(outs, 0)


def join(latter, earlier):
    d = latter.shape[0]
    both = dot_split(split(latter[:, :d]), split(earlier))
    return jnp.concatenate([both[:, :d], both[:, d:] + latter[:, d:]], 1)


def apply(step, state):
    d = state.shape[0]
    return dot_split(split(step[:, :d]), split(state)) + step[:, d:]


def middle_kernel(per, upper_ref, mine_ref, other_ref, start_ref, state_ref):
    for i in range(per):
        mine, other = mine_ref[i], other_ref[i]
        upper = upper_ref[0] != 0
        earlier = jnp.where(upper, other, mine)
        latter = jnp.where(upper, mine, other)
        state_ref[i] = apply(latter, apply(earlier, start_ref[i]))


def reach_kernel(groups, per, upper_ref, prefix_ref, before_ref, step_ref, offset_ref):
    d = before_ref.shape[1]
    row, col = iotas(d, 2 * d)
    upper = upper_ref[0] != 0
    for i in range(per):
        before = before_ref[i]
        found = [jnp.where(upper, before, jnp.where(row == col, 1.0, 0.0))]
        for place in range(1, groups):
            prefix = prefix_ref[place - 1, i]
            found.append(jnp.where(upper, join(prefix, before), prefix))
        for place in range(groups):
            step_ref[place, i] = jnp.concatenate(split(found[place][:, :d]), 1)
            offset_ref[place, i] = found[place][:, d:]


def enter_kernel(groups, per, rank_ref, later_ref, step_ref, offset_ref, start_ref, came_ref, *refs):
    out_refs, (held_ref,) = refs[:groups], refs[groups:]
    d = start_ref.shape[1]
    for i in range(per):
        high, low = split(jnp.where(later_ref[0] != 0, came_ref[i], start_ref[i]))
        for place in range(groups):
            step = step_ref[place, i]
            held_ref[place ^ rank_ref[0], i] = (
                mm(step, jnp.concatenate([high, high], 0)) + mm(step[:, :d], low) + offset_ref[place, i]
            )
    for slot in range(groups):
        out_refs[slot][...] = held_ref[slot]


def finish_heads(items, states, refs, block_hbm, flat_ref, gates_ref, inner_ref, sems):
    left_ref, right_ref, gate_ref = refs
    heads, d = left_ref.shape[0], gate_ref.shape[1]
    n = gate_ref.shape[0] // heads
    blocks = block_hbm.shape[0]
    copies = []

    def send(source, block, head, item):
        copies.append(pltpu.make_async_copy(source, block_hbm.at[block, head], sems.at[block, item]))
        copies[-1].start()

    for item, (slot, i, head) in enumerate(items):
        send(states[slot].at[i], 0, head, item)
    gates_ref[...] = gate_ref[...].astype(F32)
    for item, (slot, i, head) in enumerate(items):
        high, low = split(states[slot][i])
        left = left_ref[head]
        both = mm(left, jnp.concatenate([high, high], 0)) + mm(left[:, :d], low) + right_ref[head]
        for b in range(1, blocks):
            inner_ref[item, b - 1] = both[n + (b - 1) * d : n + b * d]
            send(inner_ref.at[item, b - 1], b, head, item)
        raw = both[:n]
        gate = gates_ref[pl.ds(head, n, stride=heads), :]
        scale = 1.0 / jnp.sqrt(jnp.mean(raw * raw, 1, keepdims=True) + EPSILON)
        flat_ref[pl.ds(head, n, stride=heads), :] = raw * scale * (gate / (1.0 + jnp.exp(-gate)))
    return copies


def slot_items(slots, per, rank):
    return [(at, i, (slot ^ rank) * per + i) for at, slot in enumerate(slots) for i in range(per)]


def first_kernel(slots, per, rank_ref, *refs):
    early = len(slots)
    states, left_ref, right_ref, gate_ref, flat_ref, block_hbm = refs[:early], *refs[early : early + 5]
    copies = finish_heads(
        slot_items(slots, per, rank_ref[0]),
        states,
        (left_ref, right_ref, gate_ref),
        block_hbm,
        flat_ref,
        *refs[early + 5 :],
    )
    for copy in copies:
        copy.wait()


def finish_kernel(slots, groups, per, rank_ref, *refs):
    states, refs = refs[: len(slots)], refs[len(slots) :]
    left_ref, right_ref, gate_ref, done_ref, _, out_hbm, block_hbm, flat_ref, *rest = refs
    *rest, rounded_ref, out_sems = rest
    copies = finish_heads(
        slot_items(slots, per, rank_ref[0]),
        states,
        (left_ref, right_ref, gate_ref),
        block_hbm,
        flat_ref,
        *rest,
    )
    heads = groups * per
    rows, d = flat_ref.shape
    head = lax.broadcasted_iota(jnp.int32, (heads, d), 0)
    slot = (head // per) ^ rank_ref[0]
    was_done = functools.reduce(jnp.logical_and, [slot != mine for mine in slots])
    size = rows // PIECES
    for at in range(PIECES):
        piece = pl.ds(at * size, size)
        whole = jnp.where(
            was_done[None],
            done_ref[piece, :].reshape(size // heads, heads, d),
            flat_ref[piece, :].reshape(size // heads, heads, d),
        )
        rounded_ref[piece, :] = whole.reshape(size, d).astype(BF16)
        copies.append(
            pltpu.make_async_copy(rounded_ref.at[piece], out_hbm.at[piece], out_sems.at[at])
        )
        copies[-1].start()
    for copy in copies:
        copy.wait()


def exact(matrix, operand):
    return jnp.einsum("...ij,...jk->...ik", matrix, operand, precision=lax.Precision.HIGHEST)


def chain(latter, earlier):
    d = latter.shape[-2]
    both = exact(latter[..., :d], earlier)
    return jnp.concatenate([both[..., :d], both[..., d:] + latter[..., d:]], -1)


def flag(value):
    return jnp.reshape(value, (1,)).astype(jnp.int32)


def on_device(
    queries, key_vectors, values, out_gate, inputs, beta_weight, log_decay, initial_state
):
    n, heads, d = queries.shape
    blocks = n // BLOCK
    count, place = lax.axis_size("seq"), lax.axis_index("seq")
    groups = math.gcd(math.gcd(4, heads), count)
    assert groups > 1
    per = heads // groups
    runs = count // groups
    rounds = runs.bit_length() - 1
    assert runs == 1 << rounds
    rank = flag(place % groups)
    run = place // groups

    def flipped(mask):
        return [(i, i ^ mask) for i in range(count)]

    def flat(tensor):
        return tensor.reshape(n * heads, d)

    pair = lax.axis_size("head") == 2
    all_heads = beta_weight.shape[0]
    zeros = call(zeros_kernel, shape(heads, d), flops=1 << 31)()
    total, cum, *logits = call(
        functools.partial(stats_kernel, heads, pair),
        [shape(heads, d), shape(heads, n)]
        + ([shape(heads, n)] * 2 if pair else [shape(all_heads, n)]),
        scratch=(pltpu.VMEM((all_heads, n), F32),) if pair else (),
        scalars=1,
        operands=5,
        flops=1 << 31,
    )(flag(lax.axis_index("head")), zeros, flat(key_vectors), beta_weight, inputs, log_decay)
    if pair:
        own, theirs = logits
        came = lax.ppermute(theirs, "head", [(0, 1), (1, 0)])
    else:
        own = lax.psum_scatter(logits[0], "head", scatter_dimension=0, tiled=True)
        came = jnp.zeros_like(own)
    packing = call(
        functools.partial(pack_kernel, groups, per),
        [shape(per, 2 * n + 8, d)] * groups + [shape(heads, n)],
        scratch=(pltpu.VMEM((n * heads, d), F32),),
        scalars=1,
        operands=5,
        flops=1 << 24,
    )
    *packs, beta = packing(rank, flat(key_vectors), flat(values), cum, own, came)

    def shared(total, mask):
        return lax.ppermute(total, "seq", flipped(mask))

    for slot in range(1, groups):
        if slot & (slot - 1) == 0:
            total = total + shared(total, slot)
    exchanged = []
    for slot in range(1, groups):
        exchanged.append(lax.ppermute(packs[slot], "seq", flipped(slot)))
    packs = [packs[0]] + exchanged
    mask = groups
    while mask < count:
        total = total + shared(total, mask)
        mask *= 2

    tokens_all = n * count
    prefix, run_map = call(
        functools.partial(run_kernel, groups, per, tokens_all),
        (shape(max(groups - 1, 1), per, d, 2 * d), shape(per, d, 2 * d)),
        scratch=(pltpu.VMEM((128, n), F32), pltpu.VMEM((groups, per, d, 2 * d), F32)),
        scalars=1,
        operands=1 + groups,
        flops=1 << 30,
    )(rank, total, *packs)

    wu = call(
        functools.partial(own_kernel, tokens_all),
        shape(heads, n, 2 * d),
        scratch=(pltpu.VMEM((n * heads, d), F32), pltpu.VMEM((128, n), F32)),
        operands=5,
        flops=1 << 31,
    )(flat(key_vectors), flat(values), beta, total, cum)

    start = lax.dynamic_slice_in_dim(initial_state, (place % groups) * per, per, 0)

    before, upper, came, later = run_map, flag(0), start, flag(0)
    if rounds == 2:
        other = lax.ppermute(run_map, "seq", flipped(groups))
        other, wu = lax.optimization_barrier((other, wu))
        upper = flag(run & 1)
        before = other
        middle = call(
            functools.partial(middle_kernel, per), shape(per, d, d), scalars=1, operands=3
        )(upper, run_map, other, start)
    elif rounds:
        eye = jnp.broadcast_to(jnp.eye(d, 2 * d, dtype=F32), run_map.shape)
        before, upper, window = eye, flag(1), run_map
        for r in range(rounds - 1):
            other = lax.ppermute(window, "seq", flipped(groups << r))
            high = (run >> r) & 1 == 1
            before = jnp.where(high, chain(before, other), before)
            window = chain(jnp.where(high, window, other), jnp.where(high, other, window))
        middle = exact(window[..., :d], start) + window[..., d:]
    if rounds:
        mirror = [(i, (runs - 1 - i // groups) * groups + i % groups) for i in range(count)]
        came = lax.ppermute(middle, "seq", mirror)
        later = flag(run >= runs // 2)
    rows = n + (blocks - 1) * d
    left, right = call(
        output_kernel,
        (shape(heads, rows, 2 * d, dtype=BF16), shape(heads, rows, d)),
        scratch=(pltpu.VMEM((n * heads, d), F32), pltpu.VMEM((128, n), F32)),
        operands=4,
        flops=1 << 30,
    )(flat(queries), flat(key_vectors), cum, wu)
    step, offset = call(
        functools.partial(reach_kernel, groups, per),
        (shape(groups, per, d, 2 * d, dtype=BF16), shape(groups, per, d, d)),
        scalars=1,
        operands=2,
        flops=1 << 28,
    )(upper, prefix, before)
    came, left, step = lax.optimization_barrier((came, left, step))
    entries = call(
        functools.partial(enter_kernel, groups, per),
        [shape(per, d, d)] * groups,
        scratch=(pltpu.VMEM((groups, per, d, d), F32),),
        scalars=2,
        operands=4,
        flops=1 << 27,
    )(rank, later, step, offset, start, came)

    states = [entries[0]]
    for slot in range(1, groups):
        states.append(lax.ppermute(entries[slot], "seq", flipped(slot)))
    early = [slot for slot in range(groups) if slot == 0 or slot in EARLY and groups > 2]
    late = [slot for slot in range(groups) if slot not in early]

    def room(slots):
        return (
            pltpu.VMEM((n * heads, d), F32),
            pltpu.VMEM((slots * per, max(blocks - 1, 1), d, d), F32),
            pltpu.SemaphoreType.DMA((blocks, slots * per)),
        )

    anywhere = pl.BlockSpec(memory_space=pl.ANY)
    params = pltpu.CompilerParams(vmem_limit_bytes=VMEM_LIMIT)
    cost = pl.CostEstimate(flops=1 << 28, bytes_accessed=1 << 20, transcendentals=0)
    done, block_states = pl.pallas_call(
        functools.partial(first_kernel, early, per),
        out_shape=(shape(n * heads, d), shape(blocks, heads, d, d)),
        in_specs=[smem()] + vmem(len(early) + 3),
        out_specs=(vmem(1)[0], anywhere),
        scratch_shapes=room(len(early)),
        compiler_params=params,
        cost_estimate=cost,
        name="first",
    )(rank, *(states[slot] for slot in early), left, right, flat(out_gate))
    gated, block_states = pl.pallas_call(
        functools.partial(finish_kernel, late, groups, per),
        out_shape=(shape(n * heads, d, dtype=BF16), shape(blocks, heads, d, d)),
        in_specs=[smem()] + vmem(len(late) + 4) + [anywhere],
        out_specs=(anywhere, anywhere),
        scratch_shapes=(pltpu.VMEM((n * heads, d), F32),)
        + room(len(late))
        + (pltpu.VMEM((n * heads, d), BF16), pltpu.SemaphoreType.DMA((PIECES,))),
        input_output_aliases={len(late) + 5: 1},
        compiler_params=params,
        cost_estimate=cost,
        name="finish",
    )(rank, *(states[slot] for slot in late), left, right, flat(out_gate), done, block_states)
    return (gated.reshape(n, heads, d), block_states)


def solution(mesh):
    return jax.shard_map(
        on_device,
        mesh=mesh,
        in_specs=(
            P("seq", "head", None),
            P("seq", "head", None),
            P("seq", "head", None),
            P("seq", "head", None),
            P("seq", "head"),
            P(None, "head"),
            P("head", "seq"),
            P("head", None, None),
        ),
        out_specs=(P("seq", "head", None), P("seq", "head", None, None)),
        check_vma=False,
    )
```
